128 devices in a mesh: row: 16 (over y, z), col: 8 (over x, core).
Axes of the slice: x: 4, y: 4, z: 4, core: 2. Of those that a mesh axis runs over, the one named last changes fastest.
Arguments:
- packed: bfloat16 [8192, 2560], P('row', 'col'), may hold values from -54 to 54
- deal_order: int32 [256], replicated, may hold values from 0 to 255, as said below
- lengths: int32 [4], replicated, may hold values from 682 to 4096, as said below
- segment_ids: int32 [8192], replicated, may hold values from -1 to 3, as said below
- page_table: int32 [64], replicated, may hold values from 0 to 63, as said below
- attn_gain: float32 [2560], replicated, may hold values from 0.1 to 1.9
- query_gain: float32 [128], replicated, may hold values from 0.1 to 1.9
- key_gain: float32 [128], replicated, may hold values from 0.1 to 1.9
- w_query: bfloat16 [2560, 4096], P('row', 'col'), may hold values from -0.125 to 0.125
- w_key: bfloat16 [2560, 1024], P('row', 'col'), may hold values from -0.125 to 0.125
- w_value: bfloat16 [2560, 1024], P('row', 'col'), may hold values from -0.125 to 0.125
- w_out: bfloat16 [4096, 2560], P('col', 'row'), may hold values from -1.5 to 1.5
Outputs:
- hidden: float32 [8192, 2560], P('row', 'col')
- kv_cache: bfloat16 [64, 8, 128, 256], P('row', 'col')
The draws below stay inside these ranges and needn't reach their ends.
Inputs may be any that keep to these rules, and one draw needn't show every extreme that they name: `lengths`: one prompt has exactly 4096 tokens; all together have fewer than 8192. `segment_ids`: prompts are packed in order from token 0: token t carries r when it lies in the r-th prompt; tokens after the last prompt carry -1. `deal_order`: a permutation of the 256 blocks; the blocks of each aligned run of 512 tokens of packed go one to each aligned run of 512 tokens of hidden, so each run of hidden takes one block from each run of packed. `page_table`: a permutation of the pages; the 4 pages of one aligned run of 512 tokens take slots in distinct aligned runs of 4 slots.
All inputs are finite; a program needn't handle non-finite values.
Results may differ from the reference program's by a relative error of at most 0.013.
Values may be sent and summed in bfloat16 or wider, within the bound.
A program may use at most 64 MiB of HBM per device.

```python
import math
import jax
import jax.numpy as jnp
from jax import lax

D = 2560
HEADS = 32
KV_HEADS = 8
HD = 128
TOK_DEV = 512
PAGE = 128
NREQ = 4
TOKENS = 8192
MAXLEN = 4096
BLK = 32
NBLK = 256
NPAGES = 64
GROUPS = 8


def request_layout(key):
    folded = jax.random.fold_in(key, 11)
    key_len, key_pick = jax.random.split(folded)
    spread = (TOKENS - MAXLEN - 1) // (2 * (NREQ - 1))
    others = jax.random.randint(key_len, (NREQ,), spread, 2 * spread + 1, dtype=jnp.int32)
    longest = jax.random.randint(key_pick, (), 0, NREQ, dtype=jnp.int32)
    lengths = jnp.where(jnp.arange(NREQ, dtype=jnp.int32) == longest, MAXLEN, others).astype(jnp.int32)
    run_ends = jnp.cumsum(lengths).astype(jnp.int32)
    places = jnp.arange(TOKENS, dtype=jnp.int32)
    before = jnp.sum((places[:, None] >= run_ends[None, :]).astype(jnp.int32), axis=1)
    segments = jnp.where(before < NREQ, before, -1).astype(jnp.int32)
    return (lengths, segments)


def draw_lengths(key, part):
    return request_layout(key)[0]


def draw_segment_ids(key, part):
    return request_layout(key)[1]


def force_target(mapping, source, wanted):
    holder = jnp.argmax(mapping == wanted).astype(jnp.int32)
    previous = mapping[source]
    return mapping.at[holder].set(previous).at[source].set(wanted).astype(jnp.int32)


def draw_page_table(key, part):
    folded = jax.random.fold_in(key, 37)
    key_map, key_slot, key_first = jax.random.split(folded, 3)
    runs = TOKENS // TOK_DEV
    per_run = TOK_DEV // PAGE
    mapping = jax.random.permutation(key_map, runs).astype(jnp.int32)
    first = jax.random.randint(key_first, (), 0, runs, dtype=jnp.int32)
    mapping = force_target(mapping, first, (first + 1) % runs)
    second = (first + 2) % runs
    mapping = force_target(mapping, second, (second + runs // 2) % runs)

    def shuffle(single):
        return jax.random.permutation(single, per_run)
    slot_perm = jax.vmap(shuffle)(jax.random.split(key_slot, runs)).astype(jnp.int32)
    which = jnp.arange(per_run, dtype=jnp.int32)[None, :]
    target = (mapping[:, None] + which) % runs
    which_full = jnp.broadcast_to(which, target.shape)
    slot = target * per_run + slot_perm[target, which_full]
    return slot.reshape(-1).astype(jnp.int32)


def draw_deal_order(key, part):
    folded = jax.random.fold_in(key, 23)
    key_src, key_dst = jax.random.split(folded)
    devices = TOKENS // TOK_DEV

    def shuffle(single):
        return jax.random.permutation(single, devices)
    src_perm = jax.vmap(shuffle)(jax.random.split(key_src, devices)).astype(jnp.int32)
    dst_perm = jax.vmap(shuffle)(jax.random.split(key_dst, devices)).astype(jnp.int32)
    dest_dev = jnp.arange(devices, dtype=jnp.int32)[:, None]
    source = jnp.arange(devices, dtype=jnp.int32)[None, :]
    target = dest_dev * devices + dst_perm
    block_id = source * devices + jnp.transpose(src_perm)
    return jnp.zeros((devices * devices,), jnp.int32).at[target.reshape(-1)].set(block_id.reshape(-1))


def draw_packed(key, part):
    key_noise, key_rows, key_cols = jax.random.split(key, 3)
    values = jnp.clip(jax.random.normal(key_noise, (TOKENS, D), jnp.float32), -6.0, 6.0)
    lower_end = 0.3
    upper_end = 3.0
    row_scale = jnp.exp(jax.random.uniform(key_rows, (TOKENS, 1), jnp.float32, math.log(lower_end), math.log(upper_end)))
    col_scale = jnp.exp(jax.random.uniform(key_cols, (1, D), jnp.float32, math.log(lower_end), math.log(upper_end)))
    return (values * row_scale * col_scale).astype(jnp.bfloat16)


def shard_levels(key, shape, cuts, low, high):
    def one(axis_at, blocks):
        draws = jax.random.uniform(jax.random.fold_in(jax.random.fold_in(key, 6), axis_at), (blocks,), jnp.float32, low / len(cuts), high / len(cuts))
        return jnp.repeat(jnp.exp(draws), shape[axis_at] // blocks).reshape((-1,) + (1,) * (len(shape) - axis_at - 1))

    level = one(*cuts[0])
    for cut in cuts[1:]:
        level = level * one(*cut)
    return level


def noise(key, dims, scale, bound, pieces=(), kind=jnp.bfloat16):
    result = scale * jax.random.normal(key, dims, jnp.float32)
    if pieces:
        result = result * shard_levels(key, dims, pieces, -0.22, 0.18)
    return jnp.clip(result, -bound, bound).astype(kind)


def setup_inputs(seed: int = 0) -> dict:
    arg_keys = jax.random.split(jax.random.key(seed), 13)
    packed = draw_packed(jax.random.fold_in(arg_keys[12], 71), 0)
    deal_order = draw_deal_order(jax.random.fold_in(arg_keys[12], 71), 0)
    lengths = draw_lengths(jax.random.fold_in(arg_keys[12], 71), 0)
    segment_ids = draw_segment_ids(jax.random.fold_in(arg_keys[12], 71), 0)
    page_table = draw_page_table(jax.random.fold_in(arg_keys[12], 71), 0)
    attn_gain = jnp.clip(1.0 + 0.18 * jax.random.normal(arg_keys[5], (D,), jnp.float32), 0.1, 1.9)
    query_gain = jnp.clip(1.0 + 0.18 * jax.random.normal(arg_keys[6], (HD,), jnp.float32), 0.1, 1.9)
    key_gain = jnp.clip(1.0 + 0.18 * jax.random.normal(arg_keys[7], (HD,), jnp.float32), 0.1, 1.9)
    w_query = noise(arg_keys[8], (D, HEADS * HD), D ** -0.5, 0.125, ((0, 16), (1, 8)))
    w_key = noise(arg_keys[9], (D, KV_HEADS * HD), D ** -0.5, 0.125, ((0, 16), (1, 8)))
    w_value = noise(arg_keys[10], (D, KV_HEADS * HD), D ** -0.5, 0.125, ((0, 16), (1, 8)))
    w_out = noise(arg_keys[11], (HEADS * HD, D), (16.0 / (HEADS * HD) ** 0.5), 1.5, ((0, 8), (1, 16)))
    return dict(packed=packed, deal_order=deal_order, lengths=lengths, segment_ids=segment_ids, page_table=page_table, attn_gain=attn_gain, query_gain=query_gain, key_gain=key_gain, w_query=w_query, w_key=w_key, w_value=w_value, w_out=w_out)


EPS = 1e-06
THETA_LOG = math.log(1000000.0)

def rms_scale(values, gain):
    mean_sq = lax.optimization_barrier(jnp.mean(values * values, axis=-1, keepdims=True))
    return values * lax.rsqrt(mean_sq + EPS) * gain

def token_positions(segment_ids, lengths):
    starts = (jnp.cumsum(lengths) - lengths).astype(jnp.int32)
    labels = jnp.arange(lengths.shape[0], dtype=jnp.int32)
    belongs = segment_ids[:, None] == labels[None, :]
    offset = lax.optimization_barrier(jnp.sum(jnp.where(belongs, starts[None, :], 0), axis=1)).astype(jnp.int32)
    return (jnp.arange(segment_ids.shape[0], dtype=jnp.int32) - offset).astype(jnp.int32)

def rope_tables(positions, head_dim):
    half_dim = head_dim // 2
    frequency = jnp.exp(jnp.arange(half_dim, dtype=jnp.float32) * (-2.0 * THETA_LOG / head_dim))
    angles = positions.astype(jnp.float32)[:, None] * frequency[None, :]
    return (jnp.cos(angles), jnp.sin(angles))

def rotate(values, cos_table, sin_table):
    half_dim = values.shape[-1] // 2
    leading = values[..., :half_dim]
    trailing = values[..., half_dim:]
    return jnp.concatenate([leading * cos_table - trailing * sin_table, trailing * cos_table + leading * sin_table], axis=-1)

def finish_heads(weighted, norm_sum, query_seg):
    valid = query_seg >= 0
    denom = jnp.where(valid[:, None, None], jnp.transpose(norm_sum, (2, 0, 1)), 1.0)
    mixed = jnp.where(valid[:, None, None, None], weighted / denom[..., None], 0.0)
    return mixed.astype(jnp.bfloat16).reshape(weighted.shape[0], -1)

def reference(packed, deal_order, lengths, segment_ids, page_table, attn_gain, query_gain, key_gain, w_query, w_key, w_value, w_out):
    group_size = HEADS // KV_HEADS
    widened = packed.astype(jnp.float32)
    normed = rms_scale(widened, attn_gain).astype(jnp.bfloat16)
    query_acc = jnp.dot(normed, w_query, preferred_element_type=jnp.float32)
    key_acc = jnp.dot(normed, w_key, preferred_element_type=jnp.float32)
    values = jnp.dot(normed, w_value, preferred_element_type=jnp.float32).astype(jnp.bfloat16).reshape(TOKENS, KV_HEADS, HD)
    positions = token_positions(segment_ids, lengths)
    cos_table, sin_table = rope_tables(positions, HD)
    rot_query = rotate(rms_scale(query_acc.reshape(TOKENS, KV_HEADS, group_size, HD), query_gain), cos_table[:, None, None, :], sin_table[:, None, None, :]).astype(jnp.bfloat16)
    rot_key = rotate(rms_scale(key_acc.reshape(TOKENS, KV_HEADS, HD), key_gain), cos_table[:, None, :], sin_table[:, None, :]).astype(jnp.bfloat16)
    block_len = math.gcd(TOKENS, 512)
    block_total = TOKENS // block_len
    score_scale = 1.0 / math.sqrt(HD)

    def query_block(block_num):
        row_start = (block_num * block_len).astype(jnp.int32)
        query_rows = lax.dynamic_slice_in_dim(rot_query, row_start, block_len, 0)
        query_seg = lax.dynamic_slice_in_dim(segment_ids, row_start, block_len, 0)
        query_pos = lax.dynamic_slice_in_dim(positions, row_start, block_len, 0)

        def key_step(key_num, acc_state):
            key_start = (key_num * block_len).astype(jnp.int32)
            key_rows = lax.dynamic_slice_in_dim(rot_key, key_start, block_len, 0)
            value_rows = lax.dynamic_slice_in_dim(values, key_start, block_len, 0)
            key_seg = lax.dynamic_slice_in_dim(segment_ids, key_start, block_len, 0)
            key_pos = lax.dynamic_slice_in_dim(positions, key_start, block_len, 0)
            allowed = (query_seg[:, None] == key_seg[None, :]) & (query_seg[:, None] >= 0) & (key_pos[None, :] <= query_pos[:, None])

            def accumulate(partials):
                weighted, norm_sum = partials
                scores = jnp.einsum('qgmd,kgd->gmqk', query_rows.astype(jnp.float32), key_rows.astype(jnp.float32)) * score_scale
                weights = jnp.where(allowed[None, None], jnp.exp(scores), 0.0).astype(jnp.bfloat16)
                weights = lax.optimization_barrier(weights).astype(jnp.float32)
                weighted = weighted + jnp.einsum('gmqk,kgd->qgmd', weights, value_rows.astype(jnp.float32))
                norm_sum = norm_sum + lax.optimization_barrier(jnp.sum(weights, axis=-1))
                return (weighted, norm_sum)

            def unchanged(partials):
                return partials
            return lax.cond(jnp.any(allowed), accumulate, unchanged, acc_state)
        start_state = (jnp.zeros((block_len, KV_HEADS, group_size, HD), jnp.float32), jnp.zeros((KV_HEADS, group_size, block_len), jnp.float32))
        weighted, norm_sum = lax.fori_loop(0, block_total, key_step, start_state)
        return finish_heads(weighted, norm_sum, query_seg)
    attended = lax.map(query_block, jnp.arange(block_total, dtype=jnp.int32)).reshape(TOKENS, HEADS * HD)
    group_width = HEADS * HD // GROUPS
    branch = jnp.zeros((TOKENS, D), jnp.float32)
    for part_num in range(GROUPS):
        partial_value = jnp.dot(attended[:, part_num * group_width:(part_num + 1) * group_width], w_out[part_num * group_width:(part_num + 1) * group_width], preferred_element_type=jnp.float32).astype(jnp.bfloat16)
        branch = branch + lax.optimization_barrier(partial_value).astype(jnp.float32)
    residual = widened + branch
    reordered = jnp.take(residual.reshape(NBLK, BLK, D), deal_order, axis=0).reshape(TOKENS, D)
    kv_rows = jnp.concatenate([rot_key, values], axis=-1)
    page_rows = jnp.transpose(kv_rows.reshape(NPAGES, PAGE, KV_HEADS, 2 * HD), (0, 2, 1, 3))
    kv_cache = jnp.zeros_like(page_rows).at[page_table].set(page_rows)
    return (reordered, kv_cache)
```

```python
import functools
import math

import jax
import jax.numpy as jnp
import numpy as np
from jax import lax
from jax.experimental import pallas as pl
from jax.experimental.pallas import tpu as pltpu
from jax.sharding import PartitionSpec as P

MESH = pl.DeviceIdType.MESH
F32 = jnp.float32
BF16 = jnp.bfloat16
EPS = 1e-06
THETA_LOG = math.log(1000000.0)
ROWS = 16
COLS = 8
BLK = 32
RUN = 512
HD = 128
FEAT = 320
WROW = 160
NCOPY = 32


def place():
    row = lax.axis_index("row")
    col = lax.axis_index("col")
    return lax.div(row, 4), lax.rem(row, 4), lax.div(col, 2), lax.rem(col, 2)


def wrap(value):
    return lax.rem(value + 4, 4)


class Spread:
    def __init__(self, view, send_sem, recv_sem):
        y, z, x, c = place()
        self.view, self.ss, self.rs = view, send_sem, recv_sem
        self.row = lambda dy, dz: wrap(y + dy) * 4 + wrap(z + dz)
        dev = lambda dy, dz: (self.row(dy, dz), 2 * x + c)
        self.dirs = {"zp": dev(0, 1), "zm": dev(0, -1), "yp": dev(1, 0), "ym": dev(-1, 0)}
        shift = {"zp": (0, -1), "zm": (0, 1), "yp": (-1, 0), "ym": (1, 0)}
        plan = [
            ("zp", (0, 0), None, None), ("zm", (0, 0), None, None),
            ("yp", (0, 0), None, None), ("ym", (0, 0), None, None),
            ("zp", (0, -1), None, 0), ("yp", (0, -1), 0, None), ("ym", (0, -1), 0, None),
            ("zm", (0, 1), None, 1), ("yp", (0, 1), 0, None), ("ym", (0, 1), 0, None),
            ("yp", (-1, 0), None, 0), ("zp", (-1, 0), 1, None), ("zm", (-1, 0), 1, None),
            ("ym", (1, 0), None, 1), ("zp", (1, 0), 1, None), ("zm", (1, 0), 1, None),
            ("yp", (0, 2), 0, None), ("ym", (0, 2), 0, None),
            ("zp", (2, 0), 1, None), ("zm", (2, 0), 1, None),
            ("yp", (-1, -1), 0, 0), ("yp", (-1, 1), 0, 0), ("yp", (-1, 2), 0, 0),
            ("ym", (1, -1), 0, 1), ("ym", (1, 1), 0, 1), ("ym", (1, 2), 0, 1),
            ("zp", (-1, -1), 1, 0), ("zp", (1, -1), 1, 0), ("zp", (2, -1), 1, 0),
            ("zm", (-1, 1), 1, 1), ("zm", (1, 1), 1, 1), ("zm", (2, 1), 1, 1),
        ]
        self.out, self.inn = [], []
        for k, (way, (dy, dz), half, quarter) in enumerate(plan):
            sy, sz = shift[way]
            sent = view(self.row(dy, dz), half, quarter)
            got = view(self.row(dy + sy, dz + sz), half, quarter)
            for refs, copies in ((sent, self.out), (got, self.inn)):
                copies.append(
                    pltpu.make_async_remote_copy(
                        src_ref=refs, dst_ref=refs, send_sem=send_sem.at[k], recv_sem=recv_sem.at[k],
                        device_id=self.dirs[way], device_id_type=MESH,
                    )
                )

    def send(self, *ks):
        for k in ks:
            self.out[k].start()

    def take(self, *ks):
        for k in ks:
            self.inn[k].wait_recv()

    def s0(self):
        self.send(0, 1, 2, 3)

    def s1(self):
        self.take(0)
        self.send(4, 5, 6)
        self.take(2)
        self.send(10, 11, 12)
        self.take(1)
        self.send(7, 8, 9)
        self.take(3)
        self.send(13, 14, 15)

    def s2(self):
        self.take(4, 7)
        self.send(16, 17)
        self.take(10, 13)
        self.send(18, 19)

    def s3(self):
        for got, sent in ((5, 20), (11, 26), (6, 23), (12, 29), (8, 21), (14, 27), (9, 24), (15, 30)):
            self.take(got)
            self.send(sent)

    def s4(self):
        for got, sent in ((16, 22), (18, 28), (17, 25), (19, 31)):
            self.take(got)
            self.send(sent)

    def s5(self):
        self.take(*range(20, 32))

    def finish(self):
        for copy in self.out:
            copy.wait_send()


def project_kernel(
    block_ref, len_ref, packed_ref, gain_ref, qgain_ref, kgain_ref, freq_ref, wq_ref, wk_ref, wv_ref,
    kv_ref, q_ref, xown_ref,
    sendbuf, xall, nrm, wq_all, wkv_all, kv_own, cos_ref, sin_ref,
    a2a_s, a2a_r, x_s, x_r, kvw_s, kvw_r, qw_s, qw_r, kv_s, kv_r, loc,
):
    me = lax.axis_index("row")
    my_col = lax.axis_index("col")
    y, z, x, c = place()
    peer = lambda k: (lax.rem(me + k, ROWS), my_col)
    xdev = lambda dx: (me, wrap(x + dx) * 2 + c)
    sibling = (me, 2 * x + 1 - c)

    barrier = pltpu.get_barrier_semaphore()
    for k in range(1, ROWS):
        pl.semaphore_signal(barrier, inc=1, device_id=peer(k), device_id_type=MESH)
    for other in (xdev(1), xdev(-1), sibling):
        pl.semaphore_signal(barrier, inc=1, device_id=other, device_id_type=MESH)

    own_rows = pl.ds(pl.multiple_of(me * WROW, WROW), WROW)
    local = [
        pltpu.make_async_copy(wk_ref, wkv_all.at[own_rows, pl.ds(0, HD)], loc.at[0]),
        pltpu.make_async_copy(wv_ref, wkv_all.at[own_rows, pl.ds(HD, HD)], loc.at[1]),
        pltpu.make_async_copy(wq_ref, wq_all.at[own_rows, :], loc.at[2]),
    ]
    for copy in local:
        copy.start()
    for d in range(ROWS):
        sendbuf[d] = packed_ref[block_ref[me, d]]
    xall[my_col, me] = sendbuf[me]
    for copy in local:
        copy.wait()
    pl.semaphore_wait(barrier, ROWS - 1 + 3)

    a2a = []
    for k in range(1, ROWS):
        to = peer(k)
        copy = pltpu.make_async_remote_copy(
            src_ref=sendbuf.at[to[0]], dst_ref=xall.at[my_col, me], send_sem=a2a_s.at[k], recv_sem=a2a_r.at[k],
            device_id=to, device_id_type=MESH,
        )
        copy.start()
        a2a.append(copy)

    def rows_view(buffer, width):
        def view(row, half, quarter):
            first, count = (0, WROW) if quarter is None else (quarter * (WROW // 2), WROW // 2)
            lane, lanes = (0, 2 * width) if half is None else (half * width, width)
            start = pl.multiple_of(row * WROW + first, WROW // 2)
            return buffer.at[pl.ds(start, count), pl.ds(lane, lanes)]

        return view

    def kv_view(row, half, quarter):
        first, count = (0, ROWS) if quarter is None else (quarter * 8, 8)
        lane, lanes = (0, 2 * HD) if half is None else (half * HD, HD)
        return kv_ref.at[pl.ds(first, count), row, :, pl.ds(lane, lanes)]

    wkv = Spread(rows_view(wkv_all, HD), kvw_s, kvw_r)
    wqs = Spread(rows_view(wq_all, 2 * HD), qw_s, qw_r)
    kvs = Spread(kv_view, kv_s, kv_r)
    wkv.s0()
    wqs.s0()

    starts = [jnp.int32(0)]
    for r in range(3):
        starts.append(starts[-1] + len_ref[r])
    total = starts[-1] + len_ref[3]
    inner = lax.broadcasted_iota(jnp.int32, (BLK, HD), 0)
    lane = lax.broadcasted_iota(jnp.int32, (BLK, HD), 1)
    freq = freq_ref[...]

    def table(s, carry):
        token = s * RUN + block_ref[s, me] * BLK + inner
        begin = jnp.zeros_like(token)
        for r in range(1, 4):
            begin = jnp.where(token >= starts[r], starts[r], begin)
        begin = jnp.where(token >= total, 0, begin)
        angle = (token - begin).astype(F32) * freq
        rows = pl.ds(pl.multiple_of(s * BLK, BLK), BLK)
        cos_ref[rows, :] = jnp.cos(angle)
        sine = jnp.sin(angle)
        sin_ref[rows, :] = jnp.where(lane < HD // 2, -sine, sine)
        return carry

    for copy in a2a:
        copy.wait_recv()

    def chunk(dx, core, half):
        return xall.at[wrap(x + dx) * 2 + core, pl.ds(half * 8, 8)]

    def xcopy(k, dx, core, half, to):
        part = chunk(dx, core, half)
        return pltpu.make_async_remote_copy(
            src_ref=part, dst_ref=part, send_sem=x_s.at[k], recv_sem=x_r.at[k], device_id=to, device_id_type=MESH
        )

    xp, xm = xdev(1), xdev(-1)
    xout = [
        xcopy(0, 0, c, 0, xp), xcopy(1, 0, c, 1, xm), xcopy(2, 0, c, 1, xp), xcopy(3, 0, c, 0, xm),
        xcopy(4, -1, c, 0, xp), xcopy(5, 1, c, 1, xm),
    ]
    xin = [
        xcopy(0, -1, c, 0, xp), xcopy(1, 1, c, 1, xm), xcopy(2, -1, c, 1, xp), xcopy(3, 1, c, 0, xm),
        xcopy(4, 2, c, 0, xp), xcopy(5, 2, c, 1, xm),
    ]
    parts = ((0, 0), (0, 1), (-1, 0), (1, 1), (-1, 1), (1, 0), (2, 0), (2, 1))
    sout = [xcopy(6 + i, dx, c, half, sibling) for i, (dx, half) in enumerate(parts)]
    sin_ = [xcopy(6 + i, dx, 1 - c, half, sibling) for i, (dx, half) in enumerate(parts)]
    for k in range(4):
        xout[k].start()
    sout[0].start()
    sout[1].start()
    wkv.s1()
    wqs.s1()
    xin[0].wait_recv()
    xout[4].start()
    sout[2].start()
    xin[1].wait_recv()
    xout[5].start()
    sout[3].start()
    wkv.s2()
    wkv.s3()
    wqs.s2()
    lax.fori_loop(0, ROWS, table, 0)
    xown_ref[...] = xall[my_col]
    xin[2].wait_recv()
    sout[4].start()
    xin[3].wait_recv()
    sout[5].start()
    wkv.s4()
    wqs.s3()
    xin[4].wait_recv()
    sout[6].start()
    xin[5].wait_recv()
    sout[7].start()
    for copy in sin_:
        copy.wait_recv()

    def norm_rows(i, carry):
        slots = pl.ds(2 * i, 2)
        total_sq = jnp.zeros((2 * BLK, FEAT), F32)
        for j in range(COLS):
            part = xall[j, slots].reshape(2 * BLK, FEAT).astype(F32)
            total_sq = total_sq + part * part
        scale = lax.rsqrt(jnp.sum(total_sq, axis=-1, keepdims=True) / (COLS * FEAT) + EPS)
        for j in range(COLS):
            part = xall[j, slots].reshape(2 * BLK, FEAT).astype(F32)
            nrm[j, pl.ds(pl.multiple_of(i * 2 * BLK, 2 * BLK), 2 * BLK), :] = (part * scale * gain_ref[j]).astype(BF16)
        return carry

    lax.fori_loop(0, ROWS // 2, norm_rows, 0)
    wkv.s5()

    def rope(acc, gain, rows):
        mean_sq = jnp.mean(acc * acc, axis=-1, keepdims=True)
        head = acc * lax.rsqrt(mean_sq + EPS) * gain
        return (head * cos_ref[rows, :] + pltpu.roll(head, HD // 2, 1) * sin_ref[rows, :]).astype(BF16)

    tile = 256
    for m in range(RUN // tile):
        rows = pl.ds(m * tile, tile)
        acc = jnp.zeros((tile, 2 * HD), F32)
        for j in range(COLS):
            acc = acc + jnp.dot(nrm[j, rows, :], wkv_all[pl.ds(j * FEAT, FEAT), :], preferred_element_type=F32)
        slots = pl.ds(m * (tile // BLK), tile // BLK)
        kv_own[slots, :, :HD] = rope(acc[:, :HD], kgain_ref[...], rows).reshape(tile // BLK, BLK, HD)
        kv_own[slots, :, HD:] = acc[:, HD:].astype(BF16).reshape(tile // BLK, BLK, HD)
    own_kv = pltpu.make_async_copy(kv_own, kv_ref.at[:, me], loc.at[3])
    own_kv.start()
    own_kv.wait()
    kvs.s0()
    wqs.s4()
    wqs.s5()
    for m in range(RUN // tile):
        rows = pl.ds(m * tile, tile)
        slots = pl.ds(m * (tile // BLK), tile // BLK)
        for h in range(4):
            acc = jnp.zeros((tile, HD), F32)
            for j in range(COLS):
                acc = acc + jnp.dot(
                    nrm[j, rows, :], wq_all[pl.ds(j * FEAT, FEAT), pl.ds(h * HD, HD)], preferred_element_type=F32
                )
            q_ref[slots, pl.ds(h * BLK, BLK), :] = rope(acc, qgain_ref[...], rows).reshape(tile // BLK, BLK, HD)
    kvs.s1()
    kvs.s2()
    kvs.s3()
    kvs.s4()
    kvs.s5()
    for copy in a2a + xout + sout:
        copy.wait_send()
    for spread in (wkv, wqs, kvs):
        spread.finish()


def project(blocks, lengths, packed, gain, query_gain, key_gain, w_query, w_key, w_value):
    vmem = pl.BlockSpec(memory_space=pltpu.VMEM)
    smem = pl.BlockSpec(memory_space=pltpu.SMEM)
    hbm = pl.BlockSpec(memory_space=pl.ANY)
    half = np.exp(np.arange(HD // 2, dtype=np.float64) * (-2.0 * THETA_LOG / HD)).astype(np.float32)
    freq = jnp.asarray(np.concatenate([half, half])[None, :])
    dma = pltpu.SemaphoreType.DMA
    return pl.pallas_call(
        project_kernel,
        name="project",
        out_shape=(
            jax.ShapeDtypeStruct((ROWS, ROWS, BLK, 2 * HD), BF16),
            jax.ShapeDtypeStruct((ROWS, 4 * BLK, HD), BF16),
            jax.ShapeDtypeStruct((ROWS, BLK, FEAT), BF16),
        ),
        in_specs=[smem, smem, vmem, vmem, vmem, vmem, vmem, hbm, hbm, hbm],
        out_specs=(hbm, vmem, vmem),
        scratch_shapes=[
            pltpu.VMEM((ROWS, BLK, FEAT), BF16),
            pltpu.VMEM((COLS, ROWS, BLK, FEAT), BF16),
            pltpu.VMEM((COLS, RUN, FEAT), BF16),
            pltpu.VMEM((ROWS * WROW, 4 * HD), BF16),
            pltpu.VMEM((ROWS * WROW, 2 * HD), BF16),
            pltpu.VMEM((ROWS, BLK, 2 * HD), BF16),
            pltpu.VMEM((RUN, HD), F32),
            pltpu.VMEM((RUN, HD), F32),
            dma((ROWS,)), dma((ROWS,)),
            dma((14,)), dma((14,)),
            dma((NCOPY,)), dma((NCOPY,)),
            dma((NCOPY,)), dma((NCOPY,)),
            dma((NCOPY,)), dma((NCOPY,)),
            dma((4,)),
        ],
        compiler_params=pltpu.CompilerParams(collective_id=0, has_side_effects=True, vmem_limit_bytes=40 << 20),
    )(blocks, lengths, packed, gain, query_gain, key_gain, freq, w_query, w_key, w_value)


def attend_kernel(
    block_ref, len_ref, order_ref, page_ref, q_ref, xown_ref, kv_hbm, out_ref, cache_ref, xperm_ref,
    kv, vext, acc, sems,
):
    me = lax.axis_index("row")
    copies = [pltpu.make_async_copy(kv_hbm.at[s], kv.at[s], sems.at[s]) for s in range(ROWS)]
    for copy in copies:
        copy.start()
    acc[...] = jnp.zeros_like(acc)
    vext[:, HD:] = jnp.ones((RUN, HD), BF16)
    ends = []
    end = jnp.int32(0)
    for r in range(4):
        end = end + len_ref[r]
        ends.append(end)
    total = ends[-1]
    scale = math.log2(math.e) / math.sqrt(HD)
    lane = lax.broadcasted_iota(jnp.int32, (1, RUN), 1)
    lane_blk = lax.div(lane, BLK)
    sub = lax.broadcasted_iota(jnp.int32, (4 * BLK, 1), 0)
    inner = lax.rem(sub, BLK)

    def query_bounds(r):
        token = r * RUN + block_ref[r, me] * BLK + inner
        begin = jnp.zeros_like(token)
        for k in range(3):
            begin = jnp.where(token >= ends[k], ends[k], begin)
        begin = jnp.where(token >= total, jnp.int32(1 << 30), begin)
        return token, begin

    def key_run(s, carry):
        pltpu.make_async_copy(kv_hbm.at[s], kv.at[s], sems.at[s]).wait()
        vext[:, :HD] = kv[s, :, :, HD:].reshape(RUN, HD)
        keys = kv[s, :, :, :HD].reshape(RUN, HD)
        first = s * RUN
        token = jnp.minimum(first + RUN - 1, total - 1)
        stop = ends[3]
        for k in (2, 1, 0):
            stop = jnp.where(token < ends[k], ends[k], stop)
        last = jnp.where(first < total, lax.div(stop - 1, RUN), s - 1)
        u = jnp.zeros((1, RUN), jnp.int32)
        for d in range(ROWS):
            u = jnp.where(lane_blk == d, block_ref[s, d], u)
        u = u * BLK + lax.rem(lane, BLK) + first

        def pair(i, carry):
            slots = pl.ds(2 * i, 2)
            query = q_ref[slots].reshape(8 * BLK, HD)
            t0, b0 = query_bounds(2 * i)
            t1, b1 = query_bounds(2 * i + 1)
            t = jnp.concatenate([t0, t1], axis=0)
            b = jnp.concatenate([b0, b1], axis=0)
            scores = lax.dot_general(query, keys, (((1,), (1,)), ((), ())), preferred_element_type=F32)
            weights = jnp.where((u <= t) & (u >= b), jnp.exp2(scores * scale), 0.0).astype(BF16)
            part = jnp.dot(weights, vext[...], preferred_element_type=F32)
            acc[slots] = acc[slots] + part.reshape(2, 4 * BLK, 2 * HD)
            return carry

        lax.fori_loop(lax.div(s, 2), lax.div(last, 2) + 1, pair, 0)
        return carry

    lax.fori_loop(0, ROWS, key_run, 0)

    def finish(p, carry):
        r = lax.div(order_ref[me * ROWS + p], ROWS)
        token, begin = query_bounds(r)
        both = acc[r]
        valid = token < total
        mixed = jnp.where(valid, both[:, :HD] / jnp.where(valid, both[:, HD:], 1.0), 0.0).astype(BF16)
        rows = pl.ds(pl.multiple_of(p * BLK, BLK), BLK)
        for h in range(4):
            out_ref[rows, h * HD : (h + 1) * HD] = mixed[h * BLK : (h + 1) * BLK, :]
        xperm_ref[rows, :] = xown_ref[r]
        return carry

    lax.fori_loop(0, ROWS, finish, 0)
    for k in range(ROWS):
        index = page_ref[k]
        cache_ref[k // 4, 0, (k % 4) * BLK : (k % 4 + 1) * BLK, :] = kv[lax.div(index, ROWS), lax.rem(index, ROWS)]


def attend(blocks, lengths, order, page_index, query, xown, kv):
    vmem = pl.BlockSpec(memory_space=pltpu.VMEM)
    smem = pl.BlockSpec(memory_space=pltpu.SMEM)
    return pl.pallas_call(
        attend_kernel,
        name="attend",
        out_shape=(
            jax.ShapeDtypeStruct((RUN, 4 * HD), BF16),
            jax.ShapeDtypeStruct((4, 1, 4 * BLK, 2 * HD), BF16),
            jax.ShapeDtypeStruct((RUN, FEAT), BF16),
        ),
        in_specs=[smem, smem, smem, smem, vmem, vmem, pl.BlockSpec(memory_space=pl.ANY)],
        out_specs=(vmem, vmem, vmem),
        scratch_shapes=[
            pltpu.VMEM((ROWS, ROWS, BLK, 2 * HD), BF16),
            pltpu.VMEM((RUN, 2 * HD), BF16),
            pltpu.VMEM((ROWS, 4 * BLK, 2 * HD), F32),
            pltpu.SemaphoreType.DMA((ROWS,)),
        ],
        compiler_params=pltpu.CompilerParams(vmem_limit_bytes=40 << 20),
    )(blocks, lengths, order, page_index, query, xown, kv)


def output_kernel(att_ref, w_ref, out_ref, mine, pair_in, pair_out, ring_out, ring_in, p_s, p_r, r_s, r_r):
    row = lax.axis_index("row")
    y, z, x, c = place()
    xp = (row, wrap(x + 1) * 2 + c)
    xm = (row, wrap(x - 1) * 2 + c)
    sibling = (row, 2 * x + 1 - c)
    barrier = pltpu.get_barrier_semaphore()
    for other in (xp, xm, sibling):
        pl.semaphore_signal(barrier, inc=1, device_id=other, device_id_type=MESH)
    pl.semaphore_wait(barrier, 3)

    def product(dx, core):
        chunk = wrap(x + dx) * 2 + core
        rows = pl.ds(pl.multiple_of(chunk * FEAT, FEAT), FEAT)
        return lax.dot_general(
            w_ref[rows, :], att_ref[...], (((1,), (1,)), ((), ())), preferred_element_type=F32
        )

    order = (2, 1, 3, 0)
    to_sibling = []
    for i, dx in enumerate(order):
        pair_out[i] = product(dx, 1 - c).astype(BF16)
        copy = pltpu.make_async_remote_copy(
            src_ref=pair_out.at[i], dst_ref=pair_in.at[i], send_sem=p_s.at[i], recv_sem=p_r.at[i],
            device_id=sibling, device_id_type=MESH,
        )
        copy.start()
        to_sibling.append(copy)
    half = FEAT // 2

    def ring(k, src, dst, to):
        return pltpu.make_async_remote_copy(
            src_ref=src, dst_ref=dst, send_sem=r_s.at[k], recv_sem=r_r.at[k], device_id=to, device_id_type=MESH
        )

    low, high = pl.ds(0, half), pl.ds(half, half)
    rings = [
        ring(0, ring_out.at[0, low], ring_in.at[0, low], xp),
        ring(1, ring_out.at[0, high], ring_in.at[0, high], xm),
        ring(2, ring_out.at[1, high], ring_in.at[1, high], xp),
        ring(3, ring_out.at[2, low], ring_in.at[2, low], xm),
        ring(4, ring_out.at[1, low], ring_in.at[1, low], xp),
        ring(5, ring_out.at[2, high], ring_in.at[2, high], xm),
    ]
    mine[...] = product(2, c)
    to_sibling[0].wait_recv()
    ring_out[0] = (mine[...] + pair_in[0].astype(F32)).astype(BF16)
    rings[0].start()
    rings[1].start()
    mine[...] = product(1, c)
    to_sibling[1].wait_recv()
    ring_out[1, high] = (mine[high, :] + pair_in[1, high].astype(F32)).astype(BF16)
    rings[2].start()
    part1 = mine[low, :] + pair_in[1, low].astype(F32)
    mine[low, :] = part1
    mine2 = product(3, c)
    to_sibling[2].wait_recv()
    ring_out[2, low] = (mine2[:half] + pair_in[2, low].astype(F32)).astype(BF16)
    rings[3].start()
    mine[high, :] = mine2[half:] + pair_in[2, high].astype(F32)
    rings[0].wait_recv()
    ring_out[1, low] = (mine[low, :] + ring_in[0, low].astype(F32)).astype(BF16)
    rings[4].start()
    rings[1].wait_recv()
    ring_out[2, high] = (mine[high, :] + ring_in[0, high].astype(F32)).astype(BF16)
    rings[5].start()
    mine[...] = product(0, c)
    to_sibling[3].wait_recv()
    mine[...] = mine[...] + pair_in[3].astype(F32)
    for k in (2, 3, 4, 5):
        rings[k].wait_recv()
    out_ref[...] = mine[...] + ring_in[1].astype(F32) + ring_in[2].astype(F32)
    for copy in to_sibling + rings:
        copy.wait_send()


def project_out(attended, w_out):
    vmem = pl.BlockSpec(memory_space=pltpu.VMEM)
    dma = pltpu.SemaphoreType.DMA
    return pl.pallas_call(
        output_kernel,
        name="output",
        out_shape=jax.ShapeDtypeStruct((FEAT, RUN), F32),
        in_specs=[vmem, vmem],
        out_specs=vmem,
        scratch_shapes=[
            pltpu.VMEM((FEAT, RUN), F32),
            pltpu.VMEM((4, FEAT, RUN), BF16),
            pltpu.VMEM((4, FEAT, RUN), BF16),
            pltpu.VMEM((3, FEAT, RUN), BF16),
            pltpu.VMEM((3, FEAT, RUN), BF16),
            dma((4,)), dma((4,)), dma((6,)), dma((6,)),
        ],
        compiler_params=pltpu.CompilerParams(collective_id=1, has_side_effects=True, vmem_limit_bytes=40 << 20),
    )(attended, w_out)


def per_device(
    packed, deal_order, lengths, segment_ids, page_table, attn_gain, query_gain, key_gain, w_query, w_key, w_value,
    w_out,
):
    row = lax.axis_index("row")
    w_out_all = lax.all_gather(w_out.T, "row", axis=0, tiled=True)
    grid = deal_order.reshape(1, ROWS, ROWS)
    runs = jnp.arange(ROWS, dtype=jnp.int32)
    blocks = jnp.sum(jnp.where(grid // ROWS == runs[:, None, None], grid % ROWS, 0), axis=2)
    kv, query, xown = project(
        blocks, lengths, packed.reshape(ROWS, BLK, FEAT), attn_gain.reshape(COLS, 1, FEAT),
        query_gain.reshape(1, HD), key_gain.reshape(1, HD), w_query, w_key, w_value,
    )
    slots = row * 4 + jnp.arange(4, dtype=jnp.int32)
    pages = jnp.arange(4 * ROWS, dtype=jnp.int32)
    page = jnp.sum(jnp.where(page_table[None, :] == slots[:, None], pages[None, :], 0), axis=1)
    wanted = (page[:, None] * 4 + jnp.arange(4, dtype=jnp.int32)[None, :]).reshape(ROWS)
    found = deal_order[None, :] == wanted[:, None]
    device = jnp.sum(jnp.where(found, jnp.arange(ROWS * ROWS, dtype=jnp.int32)[None, :] // ROWS, 0), axis=1)
    attended, cache, xperm = attend(
        blocks, lengths, deal_order, (wanted // ROWS) * ROWS + device, query, xown, kv
    )
    branch = project_out(attended, w_out_all)
    hidden = xperm.astype(F32) + branch.T
    return hidden, cache


def solution(mesh):
    in_specs = (
        P("row", "col"), P(), P(), P(), P(), P(), P(), P(),
        P("row", "col"), P("row", "col"), P("row", "col"), P("col", "row"),
    )
    out_specs = (P("row", "col"), P("row", "col", None, None))
    return jax.shard_map(per_device, mesh=mesh, in_specs=in_specs, out_specs=out_specs, check_vma=False)
```

```python
import functools
import math

import jax
import jax.numpy as jnp
import numpy as np
from jax import lax
from jax.experimental import pallas as pl
from jax.experimental.pallas import tpu as pltpu
from jax.sharding import PartitionSpec as P

MESH = pl.DeviceIdType.MESH
F32 = jnp.float32
BF16 = jnp.bfloat16
EPS = 1e-06
THETA_LOG = math.log(1000000.0)
ROWS = 16
COLS = 8
BLK = 32
RUN = 512
HALF = 16
HD = 128
FEAT = 320
WROW = 160
NCOPY = 32
SCALE = math.log2(math.e) / math.sqrt(HD)


def place():
    row = lax.axis_index("row")
    col = lax.axis_index("col")
    return lax.div(row, 4), lax.rem(row, 4), lax.div(col, 2), lax.rem(col, 2)


def wrap(value):
    return lax.rem(value + 4, 4)


class Spread:
    def __init__(self, view, send_sem, recv_sem):
        y, z, x, c = place()
        self.view, self.ss, self.rs = view, send_sem, recv_sem
        self.row = lambda dy, dz: wrap(y + dy) * 4 + wrap(z + dz)
        dev = lambda dy, dz: (self.row(dy, dz), 2 * x + c)
        self.dirs = {"zp": dev(0, 1), "zm": dev(0, -1), "yp": dev(1, 0), "ym": dev(-1, 0)}
        shift = {"zp": (0, -1), "zm": (0, 1), "yp": (-1, 0), "ym": (1, 0)}
        plan = [
            ("zp", (0, 0), None, None), ("zm", (0, 0), None, None),
            ("yp", (0, 0), None, None), ("ym", (0, 0), None, None),
            ("zp", (0, -1), None, 0), ("yp", (0, -1), 0, None), ("ym", (0, -1), 0, None),
            ("zm", (0, 1), None, 1), ("yp", (0, 1), 0, None), ("ym", (0, 1), 0, None),
            ("yp", (-1, 0), None, 0), ("zp", (-1, 0), 1, None), ("zm", (-1, 0), 1, None),
            ("ym", (1, 0), None, 1), ("zp", (1, 0), 1, None), ("zm", (1, 0), 1, None),
            ("yp", (0, 2), 0, None), ("ym", (0, 2), 0, None),
            ("zp", (2, 0), 1, None), ("zm", (2, 0), 1, None),
            ("yp", (-1, -1), 0, 0), ("yp", (-1, 1), 0, 0), ("yp", (-1, 2), 0, 0),
            ("ym", (1, -1), 0, 1), ("ym", (1, 1), 0, 1), ("ym", (1, 2), 0, 1),
            ("zp", (-1, -1), 1, 0), ("zp", (1, -1), 1, 0), ("zp", (2, -1), 1, 0),
            ("zm", (-1, 1), 1, 1), ("zm", (1, 1), 1, 1), ("zm", (2, 1), 1, 1),
        ]
        self.out, self.inn = [], []
        for k, (way, (dy, dz), half, quarter) in enumerate(plan):
            sy, sz = shift[way]
            sent = view(self.row(dy, dz), half, quarter)
            got = view(self.row(dy + sy, dz + sz), half, quarter)
            for refs, copies in ((sent, self.out), (got, self.inn)):
                copies.append(
                    pltpu.make_async_remote_copy(
                        src_ref=refs, dst_ref=refs, send_sem=send_sem.at[k], recv_sem=recv_sem.at[k],
                        device_id=self.dirs[way], device_id_type=MESH,
                    )
                )

    def send(self, *ks):
        for k in ks:
            self.out[k].start()

    def take(self, *ks):
        for k in ks:
            self.inn[k].wait_recv()

    def s0(self):
        self.send(0, 1, 2, 3)

    def s1(self):
        self.take(0)
        self.send(4, 5, 6)
        self.take(2)
        self.send(10, 11, 12)
        self.take(1)
        self.send(7, 8, 9)
        self.take(3)
        self.send(13, 14, 15)

    def s2(self):
        self.take(4, 7)
        self.send(16, 17)
        self.take(10, 13)
        self.send(18, 19)

    def s3(self):
        for got, sent in ((5, 20), (11, 26), (6, 23), (12, 29), (8, 21), (14, 27), (9, 24), (15, 30)):
            self.take(got)
            self.send(sent)

    def s4(self):
        for got, sent in ((16, 22), (18, 28), (17, 25), (19, 31)):
            self.take(got)
            self.send(sent)

    def s5(self):
        self.take(*range(20, 32))

    def finish(self):
        for copy in self.out:
            copy.wait_send()


def layer_kernel(
    order_hbm, len_hbm, page_hbm, orderv_hbm, packed_hbm, gain_hbm, qgain_hbm, kgain_hbm, freq_hbm,
    wq_ref, wk_ref, wv_ref, wo_ref,
    out_ref, cache_ref,
    order_ref, len_ref, page_ref, orderv_ref, turned, packed_ref, gain_in, gain_ref, qgain_ref, kgain_ref, freq_ref,
    sendbuf, xall, nrm, wq_all, wkv_all, wo_all, kv_ref, cos_ref, sin_ref, t_ref, b_ref, u_ref, q_ref,
    kc, vx, acc_ref, att_ref, xperm_ref, mine, own, pair_in, pair_out, ring_out, ring_in,
    a2a_s, a2a_r, x_s, x_r, kvw_s, kvw_r, qw_s, qw_r, ow_s, ow_r, kv_s, kv_r, p_s, p_r, r_s, r_r, loc,
):
    me = lax.axis_index("row")
    my_col = lax.axis_index("col")
    y, z, x, c = place()
    peer = lambda k: (lax.rem(me + k, ROWS), my_col)
    xdev = lambda dx: (me, wrap(x + dx) * 2 + c)
    sibling = (me, 2 * x + 1 - c)

    own_rows = pl.ds(pl.multiple_of(me * WROW, WROW), WROW)
    moves = (
        (packed_hbm, turned), (order_hbm, order_ref), (wk_ref, wkv_all.at[own_rows, pl.ds(0, HD)]),
        (wv_ref, wkv_all.at[own_rows, pl.ds(HD, HD)]), (wq_ref, wq_all.at[own_rows, :]),
        (wo_ref, wo_all.at[own_rows, :]), (len_hbm, len_ref), (page_hbm, page_ref), (orderv_hbm, orderv_ref),
        (gain_hbm, gain_in), (qgain_hbm, qgain_ref), (kgain_hbm, kgain_ref), (freq_hbm, freq_ref),
    )
    local = [pltpu.make_async_copy(src, dst, loc.at[i]) for i, (src, dst) in enumerate(moves)]
    for copy in local:
        copy.start()
    barrier = pltpu.get_barrier_semaphore()
    for k in range(1, ROWS):
        pl.semaphore_signal(barrier, inc=1, device_id=peer(k), device_id_type=MESH)
    for other in (xdev(1), xdev(-1), sibling):
        pl.semaphore_signal(barrier, inc=1, device_id=other, device_id_type=MESH)

    local[0].wait()
    for i in range(4):
        packed_ref[4 * i : 4 * i + 4] = turned[:, i * HD : (i + 1) * HD].T.reshape(4, BLK, FEAT)
    local[1].wait()

    def fill(d, carry):
        index = jnp.int32(0)
        for p in range(ROWS):
            block = order_ref[d * ROWS + p]
            index = index + jnp.where(lax.div(block, ROWS) == me, lax.rem(block, ROWS), 0)
        sendbuf[d] = packed_ref[jnp.minimum(index, ROWS - 1)]
        return carry

    lax.fori_loop(0, ROWS, fill, 0)
    xall[my_col, me] = sendbuf[me]
    for copy in local[2:6]:
        copy.wait()
    pl.semaphore_wait(barrier, ROWS - 1 + 3)

    halves = (pl.ds(0, HALF), pl.ds(HALF, HALF))
    a2a = []
    for h in range(2):
        for k in range(1, ROWS):
            to = peer(k)
            copy = pltpu.make_async_remote_copy(
                src_ref=sendbuf.at[to[0], halves[h]], dst_ref=xall.at[my_col, me, halves[h]],
                send_sem=a2a_s.at[h, k], recv_sem=a2a_r.at[h, k], device_id=to, device_id_type=MESH,
            )
            copy.start()
            a2a.append(copy)

    def rows_view(buffer, width):
        def view(row, half, quarter):
            first, count = (0, WROW) if quarter is None else (quarter * (WROW // 2), WROW // 2)
            lane, lanes = (0, 2 * width) if half is None else (half * width, width)
            start = pl.multiple_of(row * WROW + first, WROW // 2)
            return buffer.at[pl.ds(start, count), pl.ds(lane, lanes)]

        return view

    def kv_view(h):
        def view(row, half, quarter):
            first, count = (0, ROWS) if quarter is None else (quarter * 8, 8)
            lane, lanes = (0, 2 * HD) if half is None else (half * HD, HD)
            return kv_ref.at[pl.ds(first, count), row, halves[h], pl.ds(lane, lanes)]

        return view

    wkv = Spread(rows_view(wkv_all, HD), kvw_s, kvw_r)
    wqs = Spread(rows_view(wq_all, 2 * HD), qw_s, qw_r)
    wos = Spread(rows_view(wo_all, 2 * HD), ow_s, ow_r)
    kvs = [Spread(kv_view(h), kv_s.at[h], kv_r.at[h]) for h in range(2)]
    wkv.s0()
    wqs.s0()

    for copy in local[6:]:
        copy.wait()
    flat = gain_in[...]
    rolled = pltpu.roll(flat, HD // 2, 1)
    low_lanes = lax.broadcasted_iota(jnp.int32, (1, HD), 1) < HD // 2
    for j in range(COLS):
        r = (j * FEAT) // HD
        for i in range(3):
            if j % 2 == 0:
                piece = flat[r + i : r + i + 1]
            elif r + i + 1 < flat.shape[0]:
                piece = jnp.where(low_lanes, rolled[r + i : r + i + 1], rolled[r + i + 1 : r + i + 2])
            else:
                piece = rolled[r + i : r + i + 1]
            width = min(HD, FEAT - i * HD)
            gain_ref[j : j + 1, i * HD : i * HD + width] = piece[:, :width]

    starts = [jnp.int32(0)]
    for r in range(3):
        starts.append(starts[-1] + len_ref[r])
    total = starts[-1] + len_ref[3]
    inner = lax.broadcasted_iota(jnp.int32, (BLK, HD), 0)
    lane = lax.broadcasted_iota(jnp.int32, (BLK, HD), 1)
    freq = freq_ref[...]

    def table(s, carry):
        base = jnp.int32(0)
        for p in range(ROWS):
            block = order_ref[me * ROWS + p]
            base = base + jnp.where(lax.div(block, ROWS) == s, block * BLK, 0)
        token = base + inner
        begin = jnp.zeros_like(token)
        for r in range(1, 4):
            begin = jnp.where(token >= starts[r], starts[r], begin)
        t_ref[s] = jnp.concatenate([token] * 4, axis=0)
        b_ref[s] = jnp.concatenate([jnp.where(token >= total, 1 << 30, begin)] * 4, axis=0)
        begin = jnp.where(token >= total, 0, begin)
        angle = (token - begin).astype(F32) * freq
        cos_ref[s] = jnp.cos(angle)
        sine = jnp.sin(angle)
        sin_ref[s] = jnp.where(lane < HD // 2, -sine, sine)
        return carry

    def xcopy(h, k, dx, core, first, count, to):
        part = xall.at[wrap(x + dx) * 2 + core, pl.ds(first, count), halves[h]]
        return pltpu.make_async_remote_copy(
            src_ref=part, dst_ref=part, send_sem=x_s.at[h, k], recv_sem=x_r.at[h, k], device_id=to, device_id_type=MESH
        )

    xp, xm = xdev(1), xdev(-1)
    ways = ((0, 0, 16, xp), (0, 0, 16, xm), (-1, 0, 8, xp), (1, 8, 8, xm))
    from_ = ((-1, 0, 16, xp), (1, 0, 16, xm), (2, 0, 8, xp), (2, 8, 8, xm))
    side = ((0, 0, 16), (-1, 0, 16), (1, 0, 16), (2, 0, 16))
    xout, xin, sout, sin_ = [], [], [], []
    for h in range(2):
        xout.append([xcopy(h, k, w[0], c, w[1], w[2], w[3]) for k, w in enumerate(ways)])
        xin.append([xcopy(h, k, w[0], c, w[1], w[2], w[3]) for k, w in enumerate(from_)])
        sout.append([xcopy(h, 4 + k, w[0], c, w[1], w[2], sibling) for k, w in enumerate(side)])
        sin_.append([xcopy(h, 4 + k, w[0], 1 - c, w[1], w[2], sibling) for k, w in enumerate(side)])

    def norm_rows(h):
        def body(i, carry):
            slots = pl.ds(4 * i, 4)
            total_sq = jnp.zeros((4 * HALF, FEAT), F32)
            for j in range(COLS):
                part = xall[j, slots, halves[h], :].reshape(4 * HALF, FEAT).astype(F32)
                total_sq = total_sq + part * part
            scale = lax.rsqrt(jnp.sum(total_sq, axis=-1, keepdims=True) / (COLS * FEAT) + EPS)
            for j in range(COLS):
                part = xall[j, slots, halves[h], :].reshape(4 * HALF, FEAT).astype(F32)
                rows = pl.ds(pl.multiple_of(h * 256 + i * 4 * HALF, 4 * HALF), 4 * HALF)
                nrm[j, rows, :] = (part * scale * gain_ref[j : j + 1, :]).astype(BF16)
            return carry

        lax.fori_loop(0, 4, body, 0)

    def rope(acc, gain, h):
        mean_sq = jnp.mean(acc * acc, axis=-1, keepdims=True)
        head = acc * lax.rsqrt(mean_sq + EPS) * gain
        cosine = cos_ref[:, halves[h], :].reshape(256, HD)
        sine = sin_ref[:, halves[h], :].reshape(256, HD)
        return (head * cosine + pltpu.roll(head, HD // 2, 1) * sine).reshape(ROWS, HALF, HD)

    def keys_values(h):
        acc = jnp.zeros((256, 2 * HD), F32)
        for j in range(COLS):
            acc = acc + jnp.dot(
                nrm[j, pl.ds(h * 256, 256), :], wkv_all[pl.ds(j * FEAT, FEAT), :], preferred_element_type=F32
            )
        kv_ref[:, me, halves[h], :HD] = rope(acc[:, :HD], kgain_ref[...], h).astype(BF16)
        kv_ref[:, me, halves[h], HD:] = acc[:, HD:].astype(BF16).reshape(ROWS, HALF, HD)
        kvs[h].s0()

    def queries(h):
        for g in range(4):
            acc = jnp.zeros((256, HD), F32)
            for j in range(COLS):
                acc = acc + jnp.dot(
                    nrm[j, pl.ds(h * 256, 256), :], wq_all[pl.ds(j * FEAT, FEAT), pl.ds(g * HD, HD)],
                    preferred_element_type=F32,
                )
            q_ref[:, pl.ds(g * BLK + h * HALF, HALF), :] = (rope(acc, qgain_ref[...], h) * SCALE).astype(BF16)

    for h in range(2):
        for copy in a2a[h * 15 : h * 15 + 15]:
            copy.wait_recv()
        xout[h][0].start()
        xout[h][1].start()
        sout[h][0].start()
    wkv.s1()
    wqs.s1()
    for h in range(2):
        xin[h][0].wait_recv()
        xout[h][2].start()
        sout[h][1].start()
        xin[h][1].wait_recv()
        xout[h][3].start()
        sout[h][2].start()
        if h == 0:
            wkv.s2()
            wkv.s3()
            wqs.s2()
    lax.fori_loop(0, ROWS, table, 0)
    wkv.s4()
    wqs.s3()
    xin[0][2].wait_recv()
    xin[0][3].wait_recv()
    sout[0][3].start()
    for copy in sin_[0]:
        copy.wait_recv()
    norm_rows(0)
    wqs.s4()
    wkv.s5()
    keys_values(0)
    xin[1][2].wait_recv()
    xin[1][3].wait_recv()
    sout[1][3].start()
    for copy in sin_[1]:
        copy.wait_recv()
    norm_rows(1)
    keys_values(1)
    wqs.s5()
    queries(0)
    kvs[0].s1()
    queries(1)

    vx[:, HD:] = jnp.ones((RUN, HD), BF16)
    acc_ref[...] = jnp.zeros_like(acc_ref)
    row_lane = lax.broadcasted_iota(jnp.int32, (1, RUN), 1)
    lane_slot = lax.div(row_lane, BLK)
    lane_base = lax.rem(row_lane, BLK)

    def stage(dy, dz):
        d = wrap(y + dy) * 4 + wrap(z + dz)
        kc[...] = kv_ref[:, d, :, :HD].reshape(RUN, HD)
        vx[:, :HD] = kv_ref[:, d, :, HD:].reshape(RUN, HD)
        u = jnp.zeros((1, RUN), jnp.int32)
        for p in range(ROWS):
            block = order_ref[d * ROWS + p]
            u = jnp.where(lane_slot == lax.div(block, ROWS), block * BLK, u)
        u_ref[0:1, :] = u + lane_base

    def attend():
        for quad, (first, last) in enumerate(((0, 1), (0, 2), (0, 3), (1, 4))):
            keys = kc[first * HD : last * HD, :]
            values = vx[first * HD : last * HD, :]
            for m in range(2):
                slots = pl.ds(4 * quad + 2 * m, 2)
                query = q_ref[slots].reshape(2 * HD, HD)
                scores = lax.dot_general(query, keys, (((1,), (1,)), ((), ())), preferred_element_type=F32)
                begin = b_ref[slots].reshape(2 * HD, HD)
                parts = []
                for kb in range(last - first):
                    u = u_ref[0:1, (first + kb) * HD : (first + kb + 1) * HD]
                    seen = u >= begin
                    if first + kb == last - 1:
                        seen = seen & (u <= t_ref[slots].reshape(2 * HD, HD))
                    weight = jnp.exp2(scores[:, kb * HD : (kb + 1) * HD])
                    parts.append(jnp.where(seen, weight, 0.0).astype(BF16))
                part = jnp.dot(jnp.concatenate(parts, axis=1), values, preferred_element_type=F32)
                acc_ref[slots] = acc_ref[slots] + part.reshape(2, HD, 2 * HD)

    def first_part():
        kvs[1].take(0)
        kvs[1].send(4, 5, 6)

    def second_part():
        kvs[1].take(2)
        kvs[1].send(10, 11, 12)

    def third_part():
        kvs[1].take(1)
        kvs[1].send(7, 8, 9)

    def fourth_part():
        kvs[1].take(3)
        kvs[1].send(13, 14, 15)

    turns = (
        ((0, 0),),
        ((0, -1), first_part),
        ((-1, 0), second_part),
        ((0, 1), third_part),
        ((1, 0), fourth_part, kvs[0].s2),
        ((0, 2), kvs[1].s2),
        ((2, 0), kvs[0].s3),
        ((-1, -1), kvs[1].s3, wos.s0),
        ((-1, 1), kvs[0].s4),
        ((1, -1), kvs[1].s4),
        ((1, 1),),
        ((-1, 2), kvs[0].s5, kvs[1].s5, wos.s1),
        ((1, 2),),
        ((2, -1), wos.s2),
        ((2, 1),),
        ((2, 2), wos.s3),
    )

    def turn(n, carry):
        for i, (where, *moves) in enumerate(turns):

            @pl.when(n == i)
            def _():
                for move in moves:
                    move()
                stage(*where)

        attend()
        return carry

    lax.fori_loop(0, ROWS, turn, 0)
    wos.s4()

    def finish(p, carry):
        r = lax.div(order_ref[me * ROWS + p], ROWS)
        both = acc_ref[r]
        valid = t_ref[r] < total
        mixed = jnp.where(valid, both[:, :HD] / jnp.where(valid, both[:, HD:], 1.0), 0.0).astype(BF16)
        rows = pl.ds(pl.multiple_of(p * BLK, BLK), BLK)
        for g in range(4):
            att_ref[rows, g * HD : (g + 1) * HD] = mixed[g * BLK : (g + 1) * BLK, :]
        xperm_ref[rows, :] = xall[my_col, r]
        return carry

    lax.fori_loop(0, ROWS, finish, 0)

    half = FEAT // 2
    low, high = pl.ds(0, half), pl.ds(half, half)

    def product(dx, core):
        rows = pl.ds(pl.multiple_of((wrap(x + dx) * 2 + core) * FEAT, FEAT), FEAT)
        return lax.dot_general(
            wo_all[rows, :], att_ref[...], (((1,), (1,)), ((), ())), preferred_element_type=F32
        )

    def ring(k, src, dst, to):
        return pltpu.make_async_remote_copy(
            src_ref=src, dst_ref=dst, send_sem=r_s.at[k], recv_sem=r_r.at[k], device_id=to, device_id_type=MESH
        )

    rings = [
        ring(0, ring_out.at[0, low], ring_in.at[0, low], xp),
        ring(1, ring_out.at[0, high], ring_in.at[0, high], xm),
        ring(2, ring_out.at[1, high], ring_in.at[1, high], xp),
        ring(3, ring_out.at[2, low], ring_in.at[2, low], xm),
        ring(4, ring_out.at[1, low], ring_in.at[1, low], xp),
        ring(5, ring_out.at[2, high], ring_in.at[2, high], xm),
    ]
    pairs = [
        pltpu.make_async_remote_copy(
            src_ref=pair_out.at[i], dst_ref=pair_in.at[i], send_sem=p_s.at[i], recv_sem=p_r.at[i],
            device_id=sibling, device_id_type=MESH,
        )
        for i in range(4)
    ]
    hops = (2, 1, 3, 0)

    def both(i):
        pairs[i].wait_recv()
        mine[i] = mine[i] + pair_in[i].astype(F32)

    def compute(i):
        pair_out[i] = product(hops[i], 1 - c).astype(BF16)
        pairs[i].start()
        mine[i] = product(hops[i], c)

    wos.s5()
    compute(0)
    compute(1)
    both(0)
    ring_out[0] = mine[0].astype(BF16)
    rings[0].start()
    rings[1].start()
    compute(2)
    both(1)
    ring_out[1, high] = mine[1, high].astype(BF16)
    rings[2].start()
    both(2)
    ring_out[2, low] = mine[2, low].astype(BF16)
    rings[3].start()
    compute(3)
    rings[0].wait_recv()
    ring_out[1, low] = (mine[1, low] + ring_in[0, low].astype(F32)).astype(BF16)
    rings[4].start()
    rings[1].wait_recv()
    ring_out[2, high] = (mine[2, high] + ring_in[0, high].astype(F32)).astype(BF16)
    rings[5].start()
    both(3)
    for i in range(4):
        columns = pl.ds(i * HD, HD)
        own[:, columns] = mine[3, :, columns] + xperm_ref[columns, :].T.astype(F32)

    orders = orderv_ref[...]
    holder = lax.broadcasted_iota(jnp.int32, (2, HD), 0) * 8 + lax.div(lax.broadcasted_iota(jnp.int32, (2, HD), 1), ROWS)
    for k in range(4):
        page = lax.fori_loop(
            0, 4 * ROWS, lambda p, found: found + jnp.where(page_ref[p] == me * 4 + k, p, 0), jnp.int32(0)
        )
        for i in range(4):
            block = page * 4 + i
            device = jnp.minimum(jnp.sum(jnp.where(orders == block, holder, 0)), ROWS - 1)
            run = jnp.minimum(lax.div(block, ROWS), ROWS - 1)
            cache_ref[k, 0, i * BLK : (i + 1) * BLK, :] = kv_ref[run, device]
    for k in (2, 3, 4, 5):
        rings[k].wait_recv()
    out_ref[...] = own[...] + ring_in[1].astype(F32) + ring_in[2].astype(F32)
    for copy in a2a + xout[0] + xout[1] + sout[0] + sout[1] + pairs + rings:
        copy.wait_send()
    for spread in (wkv, wqs, wos, *kvs):
        spread.finish()


def layer(order, lengths, pages, packed, gain, query_gain, key_gain, w_query, w_key, w_value, w_out):
    vmem = pl.BlockSpec(memory_space=pltpu.VMEM)
    hbm = pl.BlockSpec(memory_space=pltpu.HBM)
    half = np.exp(np.arange(HD // 2, dtype=np.float64) * (-2.0 * THETA_LOG / HD)).astype(np.float32)
    freq = jnp.asarray(np.concatenate([half, half])[None, :])
    dma = pltpu.SemaphoreType.DMA
    return pl.pallas_call(
        layer_kernel,
        name="layer",
        out_shape=(
            jax.ShapeDtypeStruct((FEAT, RUN), F32),
            jax.ShapeDtypeStruct((4, 1, 4 * BLK, 2 * HD), BF16),
        ),
        in_specs=[hbm] * 13,
        out_specs=(vmem, vmem),
        scratch_shapes=[
            pltpu.SMEM((ROWS * ROWS,), jnp.int32), pltpu.SMEM((4,), jnp.int32), pltpu.SMEM((4 * ROWS,), jnp.int32),
            pltpu.VMEM((2, HD), jnp.int32),
            pltpu.VMEM((FEAT, RUN), BF16), pltpu.VMEM((ROWS, BLK, FEAT), BF16),
            pltpu.VMEM((COLS * FEAT // HD, HD), F32), pltpu.VMEM((COLS, FEAT), F32),
            pltpu.VMEM((1, HD), F32), pltpu.VMEM((1, HD), F32), pltpu.VMEM((1, HD), F32),
            pltpu.VMEM((ROWS, BLK, FEAT), BF16),
            pltpu.VMEM((COLS, ROWS, BLK, FEAT), BF16),
            pltpu.VMEM((COLS, RUN, FEAT), BF16),
            pltpu.VMEM((ROWS * WROW, 4 * HD), BF16),
            pltpu.VMEM((ROWS * WROW, 2 * HD), BF16),
            pltpu.VMEM((ROWS * WROW, 4 * HD), BF16),
            pltpu.VMEM((ROWS, ROWS, BLK, 2 * HD), BF16),
            pltpu.VMEM((ROWS, BLK, HD), F32),
            pltpu.VMEM((ROWS, BLK, HD), F32),
            pltpu.VMEM((ROWS, HD, HD), jnp.int32),
            pltpu.VMEM((ROWS, HD, HD), jnp.int32),
            pltpu.VMEM((8, RUN), jnp.int32),
            pltpu.VMEM((ROWS, HD, HD), BF16),
            pltpu.VMEM((RUN, HD), BF16),
            pltpu.VMEM((RUN, 2 * HD), BF16),
            pltpu.VMEM((ROWS, HD, 2 * HD), F32),
            pltpu.VMEM((RUN, 4 * HD), BF16),
            pltpu.VMEM((RUN, FEAT), BF16),
            pltpu.VMEM((4, FEAT, RUN), F32),
            pltpu.VMEM((FEAT, RUN), F32),
            pltpu.VMEM((4, FEAT, RUN), BF16),
            pltpu.VMEM((4, FEAT, RUN), BF16),
            pltpu.VMEM((3, FEAT, RUN), BF16),
            pltpu.VMEM((3, FEAT, RUN), BF16),
            dma((2, ROWS)), dma((2, ROWS)),
            dma((2, 8)), dma((2, 8)),
            dma((NCOPY,)), dma((NCOPY,)),
            dma((NCOPY,)), dma((NCOPY,)),
            dma((NCOPY,)), dma((NCOPY,)),
            dma((2, NCOPY)), dma((2, NCOPY)),
            dma((4,)), dma((4,)), dma((6,)), dma((6,)),
            dma((13,)),
        ],
        compiler_params=pltpu.CompilerParams(collective_id=0, has_side_effects=True, vmem_limit_bytes=44 << 20),
    )(
        order, lengths, pages, order.reshape(2, HD), packed, gain, query_gain, key_gain, freq, w_query, w_key, w_value,
        w_out,
    )


def per_device(
    packed, deal_order, lengths, segment_ids, page_table, attn_gain, query_gain, key_gain, w_query, w_key, w_value,
    w_out,
):
    hidden, cache = layer(
        deal_order, lengths, page_table, packed.T, attn_gain.reshape(COLS * FEAT // HD, HD),
        query_gain.reshape(1, HD), key_gain.reshape(1, HD), w_query, w_key, w_value, w_out.T,
    )
    return hidden.T, cache


def solution(mesh):
    in_specs = (
        P("row", "col"), P(), P(), P(), P(), P(), P(), P(),
        P("row", "col"), P("row", "col"), P("row", "col"), P("col", "row"),
    )
    out_specs = (P("row", "col"), P("row", "col", None, None))
    return jax.shard_map(per_device, mesh=mesh, in_specs=in_specs, out_specs=out_specs, check_vma=False)
```

```python
import functools
import math

import jax
import jax.numpy as jnp
import numpy as np
from jax import lax
from jax.experimental import pallas as pl
from jax.experimental.pallas import tpu as pltpu
from jax.sharding import PartitionSpec as P

MESH = pl.DeviceIdType.MESH
F32 = jnp.float32
BF16 = jnp.bfloat16
EPS = 1e-06
THETA_LOG = math.log(1000000.0)
ROWS = 16
COLS = 8
BLK = 32
RUN = 512
HALF = 16
HD = 128
FEAT = 320
WROW = 160
NCOPY = 32
SCALE = math.log2(math.e) / math.sqrt(HD)


def place():
    row = lax.axis_index("row")
    col = lax.axis_index("col")
    return lax.div(row, 4), lax.rem(row, 4), lax.div(col, 2), lax.rem(col, 2)


def wrap(value):
    return lax.rem(value + 4, 4)


class Spread:
    def __init__(self, view, send_sem, recv_sem):
        y, z, x, c = place()
        self.view, self.ss, self.rs = view, send_sem, recv_sem
        self.row = lambda dy, dz: wrap(y + dy) * 4 + wrap(z + dz)
        dev = lambda dy, dz: (self.row(dy, dz), 2 * x + c)
        self.dirs = {"zp": dev(0, 1), "zm": dev(0, -1), "yp": dev(1, 0), "ym": dev(-1, 0)}
        shift = {"zp": (0, -1), "zm": (0, 1), "yp": (-1, 0), "ym": (1, 0)}
        plan = [
            ("zp", (0, 0), None, None), ("zm", (0, 0), None, None),
            ("yp", (0, 0), None, None), ("ym", (0, 0), None, None),
            ("zp", (0, -1), None, 0), ("yp", (0, -1), 0, None), ("ym", (0, -1), 0, None),
            ("zm", (0, 1), None, 1), ("yp", (0, 1), 0, None), ("ym", (0, 1), 0, None),
            ("yp", (-1, 0), None, 0), ("zp", (-1, 0), 1, None), ("zm", (-1, 0), 1, None),
            ("ym", (1, 0), None, 1), ("zp", (1, 0), 1, None), ("zm", (1, 0), 1, None),
            ("yp", (0, 2), 0, None), ("ym", (0, 2), 0, None),
            ("zp", (2, 0), 1, None), ("zm", (2, 0), 1, None),
            ("yp", (-1, -1), 0, 0), ("yp", (-1, 1), 0, 0), ("yp", (-1, 2), 0, 0),
            ("ym", (1, -1), 0, 1), ("ym", (1, 1), 0, 1), ("ym", (1, 2), 0, 1),
            ("zp", (-1, -1), 1, 0), ("zp", (1, -1), 1, 0), ("zp", (2, -1), 1, 0),
            ("zm", (-1, 1), 1, 1), ("zm", (1, 1), 1, 1), ("zm", (2, 1), 1, 1),
        ]
        self.out, self.inn = [], []
        for k, (way, (dy, dz), half, quarter) in enumerate(plan):
            sy, sz = shift[way]
            sent = view(self.row(dy, dz), half, quarter)
            got = view(self.row(dy + sy, dz + sz), half, quarter)
            for refs, copies in ((sent, self.out), (got, self.inn)):
                copies.append(
                    pltpu.make_async_remote_copy(
                        src_ref=refs, dst_ref=refs, send_sem=send_sem.at[k], recv_sem=recv_sem.at[k],
                        device_id=self.dirs[way], device_id_type=MESH,
                    )
                )

    def send(self, *ks):
        for k in ks:
            self.out[k].start()

    def take(self, *ks):
        for k in ks:
            self.inn[k].wait_recv()

    def s0(self):
        self.send(0, 1, 2, 3)

    def s1(self):
        self.take(0)
        self.send(4, 5, 6)
        self.take(2)
        self.send(10, 11, 12)
        self.take(1)
        self.send(7, 8, 9)
        self.take(3)
        self.send(13, 14, 15)

    def s2(self):
        self.take(4, 7)
        self.send(16, 17)
        self.take(10, 13)
        self.send(18, 19)

    def s3(self):
        for got, sent in ((5, 20), (11, 26), (6, 23), (12, 29), (8, 21), (14, 27), (9, 24), (15, 30)):
            self.take(got)
            self.send(sent)

    def s4(self):
        for got, sent in ((16, 22), (18, 28), (17, 25), (19, 31)):
            self.take(got)
            self.send(sent)

    def s5(self):
        self.take(*range(20, 32))

    def finish(self):
        for copy in self.out:
            copy.wait_send()


def layer_kernel(
    order_hbm, len_hbm, page_hbm, orderv_hbm, packed_hbm, gain_hbm, qgain_hbm, kgain_hbm, freq_hbm,
    wq_ref, wk_ref, wv_ref, wo_ref,
    out_ref, cache_ref,
    order_ref, len_ref, page_ref, orderv_ref, turned, packed_ref, gain_in, gain_ref, qgain_ref, kgain_ref, freq_ref,
    sendbuf, xall, nrm, wq_all, wkv_all, wo_all, kv_ref, cos_ref, sin_ref, t_ref, b_ref, u_ref, q_ref,
    kc, vx, acc_ref, att_ref, xperm_ref, mine, own, pair_in, pair_out, ring_out, ring_in,
    a2a_s, a2a_r, x_s, x_r, kvw_s, kvw_r, qw_s, qw_r, ow_s, ow_r, kv_s, kv_r, p_s, p_r, r_s, r_r, loc,
):
    me = lax.axis_index("row")
    my_col = lax.axis_index("col")
    y, z, x, c = place()
    peer = lambda k: (lax.rem(me + k, ROWS), my_col)
    xdev = lambda dx: (me, wrap(x + dx) * 2 + c)
    sibling = (me, 2 * x + 1 - c)

    own_rows = pl.ds(pl.multiple_of(me * WROW, WROW), WROW)
    moves = (
        (packed_hbm, turned), (order_hbm, order_ref), (wk_ref, wkv_all.at[own_rows, pl.ds(0, HD)]),
        (wv_ref, wkv_all.at[own_rows, pl.ds(HD, HD)]), (wq_ref, wq_all.at[own_rows, :]),
        (wo_ref, wo_all.at[own_rows, :]), (len_hbm, len_ref), (page_hbm, page_ref), (orderv_hbm, orderv_ref),
        (gain_hbm, gain_in), (qgain_hbm, qgain_ref), (kgain_hbm, kgain_ref), (freq_hbm, freq_ref),
    )
    local = [pltpu.make_async_copy(src, dst, loc.at[i]) for i, (src, dst) in enumerate(moves)]
    for copy in local:
        copy.start()
    barrier = pltpu.get_barrier_semaphore()
    for k in range(1, ROWS):
        pl.semaphore_signal(barrier, inc=1, device_id=peer(k), device_id_type=MESH)
    for other in (xdev(1), xdev(-1), sibling):
        pl.semaphore_signal(barrier, inc=1, device_id=other, device_id_type=MESH)

    local[0].wait()
    for i in range(4):
        packed_ref[4 * i : 4 * i + 4] = turned[:, i * HD : (i + 1) * HD].T.reshape(4, BLK, FEAT)
    local[1].wait()

    def fill(d, carry):
        index = jnp.int32(0)
        for p in range(ROWS):
            block = order_ref[d * ROWS + p]
            index = index + jnp.where((block >> 4) == me, (block & 15), 0)
        sendbuf[d] = packed_ref[jnp.minimum(index, ROWS - 1)]
        return carry

    lax.fori_loop(0, ROWS, fill, 0)
    xall[my_col, me] = sendbuf[me]
    for copy in local[2:6]:
        copy.wait()
    pl.semaphore_wait(barrier, ROWS - 1 + 3)

    halves = (pl.ds(0, HALF), pl.ds(HALF, HALF))
    a2a = []
    for k in range(1, ROWS):
        to = peer(k)
        copy = pltpu.make_async_remote_copy(
            src_ref=sendbuf.at[to[0]], dst_ref=xall.at[my_col, me], send_sem=a2a_s.at[k], recv_sem=a2a_r.at[k],
            device_id=to, device_id_type=MESH,
        )
        copy.start()
        a2a.append(copy)

    def rows_view(buffer, width):
        def view(row, half, quarter):
            first, count = (0, WROW) if quarter is None else (quarter * (WROW // 2), WROW // 2)
            lane, lanes = (0, 2 * width) if half is None else (half * width, width)
            start = pl.multiple_of(row * WROW + first, WROW // 2)
            return buffer.at[pl.ds(start, count), pl.ds(lane, lanes)]

        return view

    def kv_view(h):
        def view(row, half, quarter):
            first, count = (0, ROWS) if quarter is None else (quarter * 8, 8)
            lane, lanes = (0, 2 * HD) if half is None else (half * HD, HD)
            return kv_ref.at[pl.ds(first, count), row, halves[h], pl.ds(lane, lanes)]

        return view

    wkv = Spread(rows_view(wkv_all, HD), kvw_s, kvw_r)
    wqs = Spread(rows_view(wq_all, 2 * HD), qw_s, qw_r)
    wos = Spread(rows_view(wo_all, 2 * HD), ow_s, ow_r)
    kvs = [Spread(kv_view(h), kv_s.at[h], kv_r.at[h]) for h in range(2)]
    wkv.s0()
    wqs.s0()

    for copy in local[6:]:
        copy.wait()
    flat = gain_in[...]
    rolled = pltpu.roll(flat, HD // 2, 1)
    low_lanes = lax.broadcasted_iota(jnp.int32, (1, HD), 1) < HD // 2
    for j in range(COLS):
        r = (j * FEAT) // HD
        for i in range(3):
            if j % 2 == 0:
                piece = flat[r + i : r + i + 1]
            elif r + i + 1 < flat.shape[0]:
                piece = jnp.where(low_lanes, rolled[r + i : r + i + 1], rolled[r + i + 1 : r + i + 2])
            else:
                piece = rolled[r + i : r + i + 1]
            width = min(HD, FEAT - i * HD)
            gain_ref[j : j + 1, i * HD : i * HD + width] = piece[:, :width]

    starts = [jnp.int32(0)]
    for r in range(3):
        starts.append(starts[-1] + len_ref[r])
    total = starts[-1] + len_ref[3]
    inner = lax.broadcasted_iota(jnp.int32, (BLK, HD), 0)
    lane = lax.broadcasted_iota(jnp.int32, (BLK, HD), 1)
    freq = freq_ref[...]

    def table(s, carry):
        base = jnp.int32(0)
        for p in range(ROWS):
            block = order_ref[me * ROWS + p]
            base = base + jnp.where(lax.div(block, ROWS) == s, block * BLK, 0)
        token = base + inner
        begin = jnp.zeros_like(token)
        for r in range(1, 4):
            begin = jnp.where(token >= starts[r], starts[r], begin)
        t_ref[s] = jnp.concatenate([token] * 4, axis=0)
        b_ref[s] = jnp.concatenate([jnp.where(token >= total, 1 << 30, begin)] * 4, axis=0)
        begin = jnp.where(token >= total, 0, begin)
        angle = (token - begin).astype(F32) * freq
        cos_ref[s] = jnp.cos(angle)
        sine = jnp.sin(angle)
        sin_ref[s] = jnp.where(lane < HD // 2, -sine, sine)
        return carry

    def xcopy(h, k, dx, core, first, count, to):
        part = xall.at[wrap(x + dx) * 2 + core, pl.ds(first, count), halves[h]]
        return pltpu.make_async_remote_copy(
            src_ref=part, dst_ref=part, send_sem=x_s.at[h, k], recv_sem=x_r.at[h, k], device_id=to, device_id_type=MESH
        )

    xp, xm = xdev(1), xdev(-1)
    ways = ((0, 0, 16, xp), (0, 0, 16, xm), (-1, 0, 8, xp), (1, 8, 8, xm))
    from_ = ((-1, 0, 16, xp), (1, 0, 16, xm), (2, 0, 8, xp), (2, 8, 8, xm))
    side = ((0, 0, 16), (-1, 0, 16), (1, 0, 16), (2, 0, 16))
    xout, xin, sout, sin_ = [], [], [], []
    for h in range(2):
        xout.append([xcopy(h, k, w[0], c, w[1], w[2], w[3]) for k, w in enumerate(ways)])
        xin.append([xcopy(h, k, w[0], c, w[1], w[2], w[3]) for k, w in enumerate(from_)])
        sout.append([xcopy(h, 4 + k, w[0], c, w[1], w[2], sibling) for k, w in enumerate(side)])
        sin_.append([xcopy(h, 4 + k, w[0], 1 - c, w[1], w[2], sibling) for k, w in enumerate(side)])

    def norm_rows(h):
        def body(i, carry):
            slots = pl.ds(4 * i, 4)
            total_sq = jnp.zeros((4 * HALF, FEAT), F32)
            for j in range(COLS):
                part = xall[j, slots, halves[h], :].reshape(4 * HALF, FEAT).astype(F32)
                total_sq = total_sq + part * part
            scale = lax.rsqrt(jnp.sum(total_sq, axis=-1, keepdims=True) / (COLS * FEAT) + EPS)
            for j in range(COLS):
                part = xall[j, slots, halves[h], :].reshape(4 * HALF, FEAT).astype(F32)
                rows = pl.ds(pl.multiple_of(h * 256 + i * 4 * HALF, 4 * HALF), 4 * HALF)
                nrm[j, rows, :] = (part * scale * gain_ref[j : j + 1, :]).astype(BF16)
            return carry

        lax.fori_loop(0, 4, body, 0)

    def rope(acc, gain, h):
        mean_sq = jnp.mean(acc * acc, axis=-1, keepdims=True)
        head = acc * lax.rsqrt(mean_sq + EPS) * gain
        cosine = cos_ref[:, halves[h], :].reshape(256, HD)
        sine = sin_ref[:, halves[h], :].reshape(256, HD)
        return (head * cosine + pltpu.roll(head, HD // 2, 1) * sine).reshape(ROWS, HALF, HD)

    def keys_values(h):
        acc = jnp.zeros((256, 2 * HD), F32)
        for j in range(COLS):
            acc = acc + jnp.dot(
                nrm[j, pl.ds(h * 256, 256), :], wkv_all[pl.ds(j * FEAT, FEAT), :], preferred_element_type=F32
            )
        kv_ref[:, me, halves[h], :HD] = rope(acc[:, :HD], kgain_ref[...], h).astype(BF16)
        kv_ref[:, me, halves[h], HD:] = acc[:, HD:].astype(BF16).reshape(ROWS, HALF, HD)
        kvs[h].s0()

    def queries(h):
        for g in range(4):
            acc = jnp.zeros((256, HD), F32)
            for j in range(COLS):
                acc = acc + jnp.dot(
                    nrm[j, pl.ds(h * 256, 256), :], wq_all[pl.ds(j * FEAT, FEAT), pl.ds(g * HD, HD)],
                    preferred_element_type=F32,
                )
            q_ref[:, pl.ds(g * BLK + h * HALF, HALF), :] = (rope(acc, qgain_ref[...], h) * SCALE).astype(BF16)

    lax.fori_loop(0, ROWS, table, 0)
    for copy in a2a:
        copy.wait_recv()
    for h in range(2):
        xout[h][0].start()
        xout[h][1].start()
        sout[h][0].start()
    wkv.s1()
    wqs.s1()
    xin[0][0].wait_recv()
    xout[0][2].start()
    sout[0][1].start()
    xin[0][1].wait_recv()
    xout[0][3].start()
    sout[0][2].start()
    wkv.s2()
    wkv.s3()
    wqs.s2()
    xin[1][0].wait_recv()
    xout[1][2].start()
    sout[1][1].start()
    xin[1][1].wait_recv()
    xout[1][3].start()
    sout[1][2].start()
    wkv.s4()
    wqs.s3()
    wos.s0()
    xin[0][2].wait_recv()
    xin[0][3].wait_recv()
    sout[0][3].start()
    for copy in sin_[0]:
        copy.wait_recv()
    norm_rows(0)
    wkv.s5()
    keys_values(0)
    xin[1][2].wait_recv()
    xin[1][3].wait_recv()
    sout[1][3].start()
    for copy in sin_[1]:
        copy.wait_recv()
    norm_rows(1)
    keys_values(1)
    wqs.s4()
    wos.s1()
    wqs.s5()
    queries(0)
    kvs[0].s1()
    queries(1)

    vx[:, HD:] = jnp.ones((RUN, HD), BF16)
    acc_ref[...] = jnp.zeros_like(acc_ref)
    row_lane = lax.broadcasted_iota(jnp.int32, (1, RUN), 1)
    lane_slot = lax.div(row_lane, BLK)
    lane_base = lax.rem(row_lane, BLK)

    def stage(dy, dz):
        d = wrap(y + dy) * 4 + wrap(z + dz)
        kc[...] = kv_ref[:, d, :, :HD].reshape(RUN, HD)
        vx[:, :HD] = kv_ref[:, d, :, HD:].reshape(RUN, HD)
        u = jnp.zeros((1, RUN), jnp.int32)
        for p in range(ROWS):
            block = order_ref[d * ROWS + p]
            u = jnp.where(lane_slot == lax.div(block, ROWS), block * BLK, u)
        u_ref[0:1, :] = u + lane_base

    def attend():
        for quad, (first, last) in enumerate(((0, 1), (0, 2), (0, 3), (1, 4))):
            keys = kc[first * HD : last * HD, :]
            values = vx[first * HD : last * HD, :]
            for m in range(2):
                slots = pl.ds(4 * quad + 2 * m, 2)
                query = q_ref[slots].reshape(2 * HD, HD)
                scores = lax.dot_general(query, keys, (((1,), (1,)), ((), ())), preferred_element_type=F32)
                begin = b_ref[slots].reshape(2 * HD, HD)
                parts = []
                for kb in range(last - first):
                    u = u_ref[0:1, (first + kb) * HD : (first + kb + 1) * HD]
                    seen = u >= begin
                    if first + kb == last - 1:
                        seen = seen & (u <= t_ref[slots].reshape(2 * HD, HD))
                    weight = jnp.exp2(scores[:, kb * HD : (kb + 1) * HD])
                    parts.append(jnp.where(seen, weight, 0.0).astype(BF16))
                part = jnp.dot(jnp.concatenate(parts, axis=1), values, preferred_element_type=F32)
                acc_ref[slots] = acc_ref[slots] + part.reshape(2, HD, 2 * HD)

    def first_part():
        kvs[1].take(0)
        kvs[1].send(4, 5, 6)

    def second_part():
        kvs[1].take(2)
        kvs[1].send(10, 11, 12)

    def third_part():
        kvs[1].take(1)
        kvs[1].send(7, 8, 9)

    def fourth_part():
        kvs[1].take(3)
        kvs[1].send(13, 14, 15)

    def last(*ks):
        def move():
            for spread in kvs:
                spread.take(*ks)

        return move

    turns = (
        ((0, 0),),
        ((0, -1), first_part),
        ((-1, 0), second_part),
        ((0, 1), third_part),
        ((1, 0), fourth_part, kvs[0].s2),
        ((0, 2), kvs[1].s2),
        ((2, 0), kvs[0].s3),
        ((-1, -1), kvs[1].s3),
        ((-1, 1), kvs[0].s4, wos.s2),
        ((1, -1), kvs[1].s4),
        ((1, 1), wos.s3),
        ((-1, 2), last(26, 29)),
        ((2, -1), last(20, 23), wos.s4),
        ((1, 2), last(27, 30)),
        ((2, 1), last(21, 24)),
        ((2, 2), last(22, 25, 28, 31)),
    )

    def turn(n, carry):
        for i, (where, *moves) in enumerate(turns):

            @pl.when(n == i)
            def _():
                for move in moves:
                    move()
                stage(*where)

        attend()
        return carry

    lax.fori_loop(0, ROWS, turn, 0)

    def finish(p, carry):
        r = lax.div(order_ref[me * ROWS + p], ROWS)
        both = acc_ref[r]
        valid = t_ref[r] < total
        mixed = jnp.where(valid, both[:, :HD] / jnp.where(valid, both[:, HD:], 1.0), 0.0).astype(BF16)
        rows = pl.ds(pl.multiple_of(p * BLK, BLK), BLK)
        for g in range(4):
            att_ref[rows, g * HD : (g + 1) * HD] = mixed[g * BLK : (g + 1) * BLK, :]
        xperm_ref[rows, :] = xall[my_col, r]
        return carry

    lax.fori_loop(0, ROWS, finish, 0)

    half = FEAT // 2
    low, high = pl.ds(0, half), pl.ds(half, half)

    def product(dx, core):
        rows = pl.ds(pl.multiple_of((wrap(x + dx) * 2 + core) * FEAT, FEAT), FEAT)
        return lax.dot_general(
            wo_all[rows, :], att_ref[...], (((1,), (1,)), ((), ())), preferred_element_type=F32
        )

    def ring(k, src, dst, to):
        return pltpu.make_async_remote_copy(
            src_ref=src, dst_ref=dst, send_sem=r_s.at[k], recv_sem=r_r.at[k], device_id=to, device_id_type=MESH
        )

    rings = [
        ring(0, ring_out.at[0, low], ring_in.at[0, low], xp),
        ring(1, ring_out.at[0, high], ring_in.at[0, high], xm),
        ring(2, ring_out.at[1, high], ring_in.at[1, high], xp),
        ring(3, ring_out.at[2, low], ring_in.at[2, low], xm),
        ring(4, ring_out.at[1, low], ring_in.at[1, low], xp),
        ring(5, ring_out.at[2, high], ring_in.at[2, high], xm),
    ]
    pairs = [
        pltpu.make_async_remote_copy(
            src_ref=pair_out.at[i], dst_ref=pair_in.at[i], send_sem=p_s.at[i], recv_sem=p_r.at[i],
            device_id=sibling, device_id_type=MESH,
        )
        for i in range(4)
    ]
    hops = (2, 1, 3, 0)

    def both(i):
        pairs[i].wait_recv()
        mine[i] = mine[i] + pair_in[i].astype(F32)

    def compute(i):
        pair_out[i] = product(hops[i], 1 - c).astype(BF16)
        pairs[i].start()
        mine[i] = product(hops[i], c)

    wos.s5()
    compute(0)
    compute(1)
    both(0)
    ring_out[0] = mine[0].astype(BF16)
    rings[0].start()
    rings[1].start()
    compute(2)
    both(1)
    ring_out[1, high] = mine[1, high].astype(BF16)
    rings[2].start()
    both(2)
    ring_out[2, low] = mine[2, low].astype(BF16)
    rings[3].start()
    compute(3)
    rings[0].wait_recv()
    ring_out[1, low] = (mine[1, low] + ring_in[0, low].astype(F32)).astype(BF16)
    rings[4].start()
    rings[1].wait_recv()
    ring_out[2, high] = (mine[2, high] + ring_in[0, high].astype(F32)).astype(BF16)
    rings[5].start()
    both(3)
    for i in range(4):
        columns = pl.ds(i * HD, HD)
        own[:, columns] = mine[3, :, columns] + xperm_ref[columns, :].T.astype(F32)

    orders = orderv_ref[...]
    holder = lax.broadcasted_iota(jnp.int32, (2, HD), 0) * 8 + lax.div(lax.broadcasted_iota(jnp.int32, (2, HD), 1), ROWS)
    for k in range(4):
        page = lax.fori_loop(
            0, 4 * ROWS, lambda p, found: found + jnp.where(page_ref[p] == me * 4 + k, p, 0), jnp.int32(0)
        )
        for i in range(4):
            block = page * 4 + i
            device = jnp.minimum(jnp.sum(jnp.where(orders == block, holder, 0)), ROWS - 1)
            run = jnp.minimum(lax.div(block, ROWS), ROWS - 1)
            cache_ref[k, 0, i * BLK : (i + 1) * BLK, :] = kv_ref[run, device]
    for k in (2, 3, 4, 5):
        rings[k].wait_recv()
    out_ref[...] = own[...] + ring_in[1].astype(F32) + ring_in[2].astype(F32)
    for copy in a2a + xout[0] + xout[1] + sout[0] + sout[1] + pairs + rings:
        copy.wait_send()
    for spread in (wkv, wqs, wos, *kvs):
        spread.finish()


def layer(order, lengths, pages, packed, gain, query_gain, key_gain, w_query, w_key, w_value, w_out):
    vmem = pl.BlockSpec(memory_space=pltpu.VMEM)
    hbm = pl.BlockSpec(memory_space=pltpu.HBM)
    half = np.exp(np.arange(HD // 2, dtype=np.float64) * (-2.0 * THETA_LOG / HD)).astype(np.float32)
    freq = jnp.asarray(np.concatenate([half, half])[None, :])
    dma = pltpu.SemaphoreType.DMA
    return pl.pallas_call(
        layer_kernel,
        name="layer",
        out_shape=(
            jax.ShapeDtypeStruct((FEAT, RUN), F32),
            jax.ShapeDtypeStruct((4, 1, 4 * BLK, 2 * HD), BF16),
        ),
        in_specs=[hbm] * 13,
        out_specs=(vmem, vmem),
        scratch_shapes=[
            pltpu.SMEM((ROWS * ROWS,), jnp.int32), pltpu.SMEM((4,), jnp.int32), pltpu.SMEM((4 * ROWS,), jnp.int32),
            pltpu.VMEM((2, HD), jnp.int32),
            pltpu.VMEM((FEAT, RUN), BF16), pltpu.VMEM((ROWS, BLK, FEAT), BF16),
            pltpu.VMEM((COLS * FEAT // HD, HD), F32), pltpu.VMEM((COLS, FEAT), F32),
            pltpu.VMEM((1, HD), F32), pltpu.VMEM((1, HD), F32), pltpu.VMEM((1, HD), F32),
            pltpu.VMEM((ROWS, BLK, FEAT), BF16),
            pltpu.VMEM((COLS, ROWS, BLK, FEAT), BF16),
            pltpu.VMEM((COLS, RUN, FEAT), BF16),
            pltpu.VMEM((ROWS * WROW, 4 * HD), BF16),
            pltpu.VMEM((ROWS * WROW, 2 * HD), BF16),
            pltpu.VMEM((ROWS * WROW, 4 * HD), BF16),
            pltpu.VMEM((ROWS, ROWS, BLK, 2 * HD), BF16),
            pltpu.VMEM((ROWS, BLK, HD), F32),
            pltpu.VMEM((ROWS, BLK, HD), F32),
            pltpu.VMEM((ROWS, HD, HD), jnp.int32),
            pltpu.VMEM((ROWS, HD, HD), jnp.int32),
            pltpu.VMEM((8, RUN), jnp.int32),
            pltpu.VMEM((ROWS, HD, HD), BF16),
            pltpu.VMEM((RUN, HD), BF16),
            pltpu.VMEM((RUN, 2 * HD), BF16),
            pltpu.VMEM((ROWS, HD, 2 * HD), F32),
            pltpu.VMEM((RUN, 4 * HD), BF16),
            pltpu.VMEM((RUN, FEAT), BF16),
            pltpu.VMEM((4, FEAT, RUN), F32),
            pltpu.VMEM((FEAT, RUN), F32),
            pltpu.VMEM((4, FEAT, RUN), BF16),
            pltpu.VMEM((4, FEAT, RUN), BF16),
            pltpu.VMEM((3, FEAT, RUN), BF16),
            pltpu.VMEM((3, FEAT, RUN), BF16),
            dma((ROWS,)), dma((ROWS,)),
            dma((2, 8)), dma((2, 8)),
            dma((NCOPY,)), dma((NCOPY,)),
            dma((NCOPY,)), dma((NCOPY,)),
            dma((NCOPY,)), dma((NCOPY,)),
            dma((2, NCOPY)), dma((2, NCOPY)),
            dma((4,)), dma((4,)), dma((6,)), dma((6,)),
            dma((13,)),
        ],
        compiler_params=pltpu.CompilerParams(collective_id=0, has_side_effects=True, vmem_limit_bytes=44 << 20),
    )(*(pltpu.with_memory_space_constraint(a, pltpu.HBM) for a in (
        order, lengths, pages, order.reshape(2, HD), packed, gain, query_gain, key_gain, freq, w_query, w_key, w_value,
        w_out,
    )))


def per_device(
    packed, deal_order, lengths, segment_ids, page_table, attn_gain, query_gain, key_gain, w_query, w_key, w_value,
    w_out,
):
    hidden, cache = layer(
        deal_order, lengths, page_table, packed.T, attn_gain.reshape(COLS * FEAT // HD, HD),
        query_gain.reshape(1, HD), key_gain.reshape(1, HD), w_query, w_key, w_value, w_out.T,
    )
    return hidden.T, cache


def solution(mesh):
    in_specs = (
        P("row", "col"), P(), P(), P(), P(), P(), P(), P(),
        P("row", "col"), P("row", "col"), P("row", "col"), P("col", "row"),
    )
    out_specs = (P("row", "col"), P("row", "col", None, None))
    return jax.shard_map(per_device, mesh=mesh, in_specs=in_specs, out_specs=out_specs, check_vma=False)
```

```python
import functools
import math

import jax
import jax.numpy as jnp
import numpy as np
from jax import lax
from jax.experimental import pallas as pl
from jax.experimental.pallas import tpu as pltpu
from jax.sharding import PartitionSpec as P

MESH = pl.DeviceIdType.MESH
F32 = jnp.float32
BF16 = jnp.bfloat16
EPS = 1e-06
THETA_LOG = math.log(1000000.0)
ROWS = 16
COLS = 8
BLK = 32
RUN = 512
HALF = 16
HD = 128
FEAT = 320
WROW = 160
NCOPY = 32
SCALE = math.log2(math.e) / math.sqrt(HD)


def place():
    row = lax.axis_index("row")
    col = lax.axis_index("col")
    return lax.div(row, 4), lax.rem(row, 4), lax.div(col, 2), lax.rem(col, 2)


def wrap(value):
    return lax.rem(value + 4, 4)


class Spread:
    def __init__(self, view, send_sem, recv_sem):
        y, z, x, c = place()
        self.view, self.ss, self.rs = view, send_sem, recv_sem
        self.row = lambda dy, dz: wrap(y + dy) * 4 + wrap(z + dz)
        dev = lambda dy, dz: (self.row(dy, dz), 2 * x + c)
        self.dirs = {"zp": dev(0, 1), "zm": dev(0, -1), "yp": dev(1, 0), "ym": dev(-1, 0)}
        shift = {"zp": (0, -1), "zm": (0, 1), "yp": (-1, 0), "ym": (1, 0)}
        plan = [
            ("zp", (0, 0), None, None), ("zm", (0, 0), None, None),
            ("yp", (0, 0), None, None), ("ym", (0, 0), None, None),
            ("zp", (0, -1), None, 0), ("yp", (0, -1), 0, None), ("ym", (0, -1), 0, None),
            ("zm", (0, 1), None, 1), ("yp", (0, 1), 0, None), ("ym", (0, 1), 0, None),
            ("yp", (-1, 0), None, 0), ("zp", (-1, 0), 1, None), ("zm", (-1, 0), 1, None),
            ("ym", (1, 0), None, 1), ("zp", (1, 0), 1, None), ("zm", (1, 0), 1, None),
            ("yp", (0, 2), 0, None), ("ym", (0, 2), 0, None),
            ("zp", (2, 0), 1, None), ("zm", (2, 0), 1, None),
            ("yp", (-1, -1), 0, 0), ("yp", (-1, 1), 0, 0), ("yp", (-1, 2), 0, 0),
            ("ym", (1, -1), 0, 1), ("ym", (1, 1), 0, 1), ("ym", (1, 2), 0, 1),
            ("zp", (-1, -1), 1, 0), ("zp", (1, -1), 1, 0), ("zp", (2, -1), 1, 0),
            ("zm", (-1, 1), 1, 1), ("zm", (1, 1), 1, 1), ("zm", (2, 1), 1, 1),
        ]
        self.out, self.inn = [], []
        for k, (way, (dy, dz), half, quarter) in enumerate(plan):
            sy, sz = shift[way]
            sent = view(self.row(dy, dz), half, quarter)
            got = view(self.row(dy + sy, dz + sz), half, quarter)
            for refs, copies in ((sent, self.out), (got, self.inn)):
                copies.append(
                    pltpu.make_async_remote_copy(
                        src_ref=refs, dst_ref=refs, send_sem=send_sem.at[k], recv_sem=recv_sem.at[k],
                        device_id=self.dirs[way], device_id_type=MESH,
                    )
                )

    def send(self, *ks):
        for k in ks:
            self.out[k].start()

    def take(self, *ks):
        for k in ks:
            self.inn[k].wait_recv()

    def s0(self):
        self.send(0, 1, 2, 3)

    def s1(self):
        self.take(0)
        self.send(4, 5, 6)
        self.take(2)
        self.send(10, 11, 12)
        self.take(1)
        self.send(7, 8, 9)
        self.take(3)
        self.send(13, 14, 15)

    def s2(self):
        self.take(4, 7)
        self.send(16, 17)
        self.take(10, 13)
        self.send(18, 19)

    def s3(self):
        for got, sent in ((5, 20), (11, 26), (6, 23), (12, 29), (8, 21), (14, 27), (9, 24), (15, 30)):
            self.take(got)
            self.send(sent)

    def s4(self):
        for got, sent in ((16, 22), (18, 28), (17, 25), (19, 31)):
            self.take(got)
            self.send(sent)

    def s5(self):
        self.take(*range(20, 32))

    def finish(self):
        for copy in self.out:
            copy.wait_send()


def layer_kernel(
    order_hbm, len_hbm, page_hbm, orderv_hbm, packed_hbm, gain_hbm, qgain_hbm, kgain_hbm, freq_hbm,
    wq_ref, wk_ref, wv_ref, wo_ref,
    out_ref, cache_ref,
    order_ref, len_ref, page_ref, orderv_ref, turned, packed_ref, gain_in, gain_ref, qgain_ref, kgain_ref, freq_ref,
    sendbuf, xall, nrm, wq_all, wkv_all, wo_all, kv_ref, cos_ref, sin_ref, t_ref, b_ref, u_ref, q_ref,
    kc, vx, acc_ref, att_ref, xperm_ref, mine, own, pair_in, pair_out, ring_out, ring_in,
    a2a_s, a2a_r, x_s, x_r, kvw_s, kvw_r, qw_s, qw_r, ow_s, ow_r, kv_s, kv_r, p_s, p_r, r_s, r_r, loc,
):
    me = lax.axis_index("row")
    my_col = lax.axis_index("col")
    y, z, x, c = place()
    peer = lambda k: (lax.rem(me + k, ROWS), my_col)
    xdev = lambda dx: (me, wrap(x + dx) * 2 + c)
    sibling = (me, 2 * x + 1 - c)

    own_rows = pl.ds(pl.multiple_of(me * WROW, WROW), WROW)
    moves = (
        (packed_hbm, turned), (order_hbm, order_ref), (wk_ref, wkv_all.at[own_rows, pl.ds(0, HD)]),
        (wv_ref, wkv_all.at[own_rows, pl.ds(HD, HD)]), (wq_ref, wq_all.at[own_rows, :]),
        (wo_ref, wo_all.at[own_rows, :]), (len_hbm, len_ref), (page_hbm, page_ref), (orderv_hbm, orderv_ref),
        (gain_hbm, gain_in), (qgain_hbm, qgain_ref), (kgain_hbm, kgain_ref), (freq_hbm, freq_ref),
    )
    local = [pltpu.make_async_copy(src, dst, loc.at[i]) for i, (src, dst) in enumerate(moves)]
    for copy in local:
        copy.start()
    barrier = pltpu.get_barrier_semaphore()
    for k in range(1, ROWS):
        pl.semaphore_signal(barrier, inc=1, device_id=peer(k), device_id_type=MESH)
    for other in (xdev(1), xdev(-1), sibling):
        pl.semaphore_signal(barrier, inc=1, device_id=other, device_id_type=MESH)

    local[0].wait()
    for i in range(4):
        packed_ref[4 * i : 4 * i + 4] = turned[:, i * HD : (i + 1) * HD].T.reshape(4, BLK, FEAT)
    local[1].wait()

    def fill(d, carry):
        index = jnp.int32(0)
        for p in range(ROWS):
            block = order_ref[d * ROWS + p]
            index = index + jnp.where((block >> 4) == me, (block & 15), 0)
        sendbuf[d] = packed_ref[jnp.minimum(index, ROWS - 1)]
        return carry

    lax.fori_loop(0, ROWS, fill, 0)
    xall[my_col, me] = sendbuf[me]
    pl.semaphore_wait(barrier, ROWS - 1 + 3)

    halves = (pl.ds(0, HALF), pl.ds(HALF, HALF))
    a2a = []
    for k in range(1, ROWS):
        to = peer(k)
        copy = pltpu.make_async_remote_copy(
            src_ref=sendbuf.at[to[0]], dst_ref=xall.at[my_col, me], send_sem=a2a_s.at[k], recv_sem=a2a_r.at[k],
            device_id=to, device_id_type=MESH,
        )
        copy.start()
        a2a.append(copy)

    def rows_view(buffer, width):
        def view(row, half, quarter):
            first, count = (0, WROW) if quarter is None else (quarter * (WROW // 2), WROW // 2)
            lane, lanes = (0, 2 * width) if half is None else (half * width, width)
            start = pl.multiple_of(row * WROW + first, WROW // 2)
            return buffer.at[pl.ds(start, count), pl.ds(lane, lanes)]

        return view

    def kv_view(h):
        def view(row, half, quarter):
            first, count = (0, ROWS) if quarter is None else (quarter * 8, 8)
            lane, lanes = (0, 2 * HD) if half is None else (half * HD, HD)
            return kv_ref.at[pl.ds(first, count), row, halves[h], pl.ds(lane, lanes)]

        return view

    wkv = Spread(rows_view(wkv_all, HD), kvw_s, kvw_r)
    wqs = Spread(rows_view(wq_all, 2 * HD), qw_s, qw_r)
    wos = Spread(rows_view(wo_all, 2 * HD), ow_s, ow_r)
    kvs = [Spread(kv_view(h), kv_s.at[h], kv_r.at[h]) for h in range(2)]
    for copy in local[2:6]:
        copy.wait()
    wkv.s0()
    wqs.s0()

    for copy in local[6:]:
        copy.wait()
    flat = gain_in[...]
    rolled = pltpu.roll(flat, HD // 2, 1)
    low_lanes = lax.broadcasted_iota(jnp.int32, (1, HD), 1) < HD // 2
    for j in range(COLS):
        r = (j * FEAT) // HD
        for i in range(3):
            if j % 2 == 0:
                piece = flat[r + i : r + i + 1]
            elif r + i + 1 < flat.shape[0]:
                piece = jnp.where(low_lanes, rolled[r + i : r + i + 1], rolled[r + i + 1 : r + i + 2])
            else:
                piece = rolled[r + i : r + i + 1]
            width = min(HD, FEAT - i * HD)
            gain_ref[j : j + 1, i * HD : i * HD + width] = piece[:, :width]

    starts = [jnp.int32(0)]
    for r in range(3):
        starts.append(starts[-1] + len_ref[r])
    total = starts[-1] + len_ref[3]
    inner = lax.broadcasted_iota(jnp.int32, (BLK, HD), 0)
    lane = lax.broadcasted_iota(jnp.int32, (BLK, HD), 1)
    freq = freq_ref[...]

    def table(s, carry):
        base = jnp.int32(0)
        for p in range(ROWS):
            block = order_ref[me * ROWS + p]
            base = base + jnp.where(lax.div(block, ROWS) == s, block * BLK, 0)
        token = base + inner
        begin = jnp.zeros_like(token)
        for r in range(1, 4):
            begin = jnp.where(token >= starts[r], starts[r], begin)
        t_ref[s] = jnp.concatenate([token] * 4, axis=0)
        b_ref[s] = jnp.concatenate([jnp.where(token >= total, 1 << 30, begin)] * 4, axis=0)
        begin = jnp.where(token >= total, 0, begin)
        angle = (token - begin).astype(F32) * freq
        cos_ref[s] = jnp.cos(angle)
        sine = jnp.sin(angle)
        sin_ref[s] = jnp.where(lane < HD // 2, -sine, sine)
        return carry

    def xcopy(h, k, dx, core, first, count, to):
        part = xall.at[wrap(x + dx) * 2 + core, pl.ds(first, count), halves[h]]
        return pltpu.make_async_remote_copy(
            src_ref=part, dst_ref=part, send_sem=x_s.at[h, k], recv_sem=x_r.at[h, k], device_id=to, device_id_type=MESH
        )

    xp, xm = xdev(1), xdev(-1)
    ways = ((0, 0, 16, xp), (0, 0, 16, xm), (-1, 0, 8, xp), (1, 8, 8, xm))
    from_ = ((-1, 0, 16, xp), (1, 0, 16, xm), (2, 0, 8, xp), (2, 8, 8, xm))
    side = ((0, 0, 16), (-1, 0, 16), (1, 0, 16), (2, 0, 16))
    xout, xin, sout, sin_ = [], [], [], []
    for h in range(2):
        xout.append([xcopy(h, k, w[0], c, w[1], w[2], w[3]) for k, w in enumerate(ways)])
        xin.append([xcopy(h, k, w[0], c, w[1], w[2], w[3]) for k, w in enumerate(from_)])
        sout.append([xcopy(h, 4 + k, w[0], c, w[1], w[2], sibling) for k, w in enumerate(side)])
        sin_.append([xcopy(h, 4 + k, w[0], 1 - c, w[1], w[2], sibling) for k, w in enumerate(side)])

    def norm_rows(h):
        def body(i, carry):
            slots = pl.ds(4 * i, 4)
            total_sq = jnp.zeros((4 * HALF, FEAT), F32)
            for j in range(COLS):
                part = xall[j, slots, halves[h], :].reshape(4 * HALF, FEAT).astype(F32)
                total_sq = total_sq + part * part
            scale = lax.rsqrt(jnp.sum(total_sq, axis=-1, keepdims=True) / (COLS * FEAT) + EPS)
            for j in range(COLS):
                part = xall[j, slots, halves[h], :].reshape(4 * HALF, FEAT).astype(F32)
                rows = pl.ds(pl.multiple_of(h * 256 + i * 4 * HALF, 4 * HALF), 4 * HALF)
                nrm[j, rows, :] = (part * scale * gain_ref[j : j + 1, :]).astype(BF16)
            return carry

        lax.fori_loop(0, 4, body, 0)

    def rope(acc, gain, h):
        mean_sq = jnp.mean(acc * acc, axis=-1, keepdims=True)
        head = acc * lax.rsqrt(mean_sq + EPS) * gain
        cosine = cos_ref[:, halves[h], :].reshape(256, HD)
        sine = sin_ref[:, halves[h], :].reshape(256, HD)
        return (head * cosine + pltpu.roll(head, HD // 2, 1) * sine).reshape(ROWS, HALF, HD)

    def keys_values(h):
        acc = jnp.zeros((256, 2 * HD), F32)
        for j in range(COLS):
            acc = acc + jnp.dot(
                nrm[j, pl.ds(h * 256, 256), :], wkv_all[pl.ds(j * FEAT, FEAT), :], preferred_element_type=F32
            )
        kv_ref[:, me, halves[h], :HD] = rope(acc[:, :HD], kgain_ref[...], h).astype(BF16)
        kv_ref[:, me, halves[h], HD:] = acc[:, HD:].astype(BF16).reshape(ROWS, HALF, HD)
        kvs[h].s0()

    def queries(h):
        for g in range(4):
            acc = jnp.zeros((256, HD), F32)
            for j in range(COLS):
                acc = acc + jnp.dot(
                    nrm[j, pl.ds(h * 256, 256), :], wq_all[pl.ds(j * FEAT, FEAT), pl.ds(g * HD, HD)],
                    preferred_element_type=F32,
                )
            q_ref[:, pl.ds(g * BLK + h * HALF, HALF), :] = (rope(acc, qgain_ref[...], h) * SCALE).astype(BF16)

    lax.fori_loop(0, ROWS, table, 0)
    for copy in a2a:
        copy.wait_recv()
    for h in range(2):
        xout[h][0].start()
        xout[h][1].start()
        sout[h][0].start()
    wkv.s1()
    wqs.s1()
    xin[0][0].wait_recv()
    xout[0][2].start()
    sout[0][1].start()
    xin[0][1].wait_recv()
    xout[0][3].start()
    sout[0][2].start()
    wkv.s2()
    wkv.s3()
    wqs.s2()
    xin[1][0].wait_recv()
    xout[1][2].start()
    sout[1][1].start()
    xin[1][1].wait_recv()
    xout[1][3].start()
    sout[1][2].start()
    wkv.s4()
    wqs.s3()
    wos.s0()
    xin[0][2].wait_recv()
    xin[0][3].wait_recv()
    sout[0][3].start()
    for copy in sin_[0]:
        copy.wait_recv()
    norm_rows(0)
    wkv.s5()
    keys_values(0)
    xin[1][2].wait_recv()
    xin[1][3].wait_recv()
    sout[1][3].start()
    for copy in sin_[1]:
        copy.wait_recv()
    norm_rows(1)
    keys_values(1)
    wqs.s4()
    wos.s1()
    wqs.s5()
    queries(0)
    kvs[0].s1()
    queries(1)

    vx[:, HD:] = jnp.ones((RUN, HD), BF16)
    acc_ref[...] = jnp.zeros_like(acc_ref)
    row_lane = lax.broadcasted_iota(jnp.int32, (1, RUN), 1)
    lane_slot = lax.div(row_lane, BLK)
    lane_base = lax.rem(row_lane, BLK)

    def stage(dy, dz):
        d = wrap(y + dy) * 4 + wrap(z + dz)
        kc[...] = kv_ref[:, d, :, :HD].reshape(RUN, HD)
        vx[:, :HD] = kv_ref[:, d, :, HD:].reshape(RUN, HD)
        u = jnp.zeros((1, RUN), jnp.int32)
        for p in range(ROWS):
            block = order_ref[d * ROWS + p]
            u = jnp.where(lane_slot == lax.div(block, ROWS), block * BLK, u)
        u_ref[0:1, :] = u + lane_base

    def attend():
        for quad, (first, last) in enumerate(((0, 1), (0, 2), (0, 3), (1, 4))):
            keys = kc[first * HD : last * HD, :]
            values = vx[first * HD : last * HD, :]
            for m in range(2):
                slots = pl.ds(4 * quad + 2 * m, 2)
                query = q_ref[slots].reshape(2 * HD, HD)
                scores = lax.dot_general(query, keys, (((1,), (1,)), ((), ())), preferred_element_type=F32)
                begin = b_ref[slots].reshape(2 * HD, HD)
                parts = []
                for kb in range(last - first):
                    u = u_ref[0:1, (first + kb) * HD : (first + kb + 1) * HD]
                    seen = u >= begin
                    if first + kb == last - 1:
                        seen = seen & (u <= t_ref[slots].reshape(2 * HD, HD))
                    weight = jnp.exp2(scores[:, kb * HD : (kb + 1) * HD])
                    parts.append(jnp.where(seen, weight, 0.0).astype(BF16))
                part = jnp.dot(jnp.concatenate(parts, axis=1), values, preferred_element_type=F32)
                acc_ref[slots] = acc_ref[slots] + part.reshape(2, HD, 2 * HD)

    def first_part():
        kvs[1].take(0)
        kvs[1].send(4, 5, 6)

    def second_part():
        kvs[1].take(2)
        kvs[1].send(10, 11, 12)

    def third_part():
        kvs[1].take(1)
        kvs[1].send(7, 8, 9)

    def fourth_part():
        kvs[1].take(3)
        kvs[1].send(13, 14, 15)

    def last(*ks):
        def move():
            for spread in kvs:
                spread.take(*ks)

        return move

    turns = (
        ((0, 0),),
        ((0, -1), first_part),
        ((-1, 0), second_part),
        ((0, 1), third_part),
        ((1, 0), fourth_part, kvs[0].s2),
        ((0, 2), kvs[1].s2),
        ((2, 0), kvs[0].s3),
        ((-1, -1), kvs[1].s3),
        ((-1, 1), kvs[0].s4, wos.s2),
        ((1, -1), kvs[1].s4),
        ((1, 1), wos.s3),
        ((-1, 2), last(26, 29)),
        ((2, -1), last(20, 23), wos.s4),
        ((1, 2), last(27, 30)),
        ((2, 1), last(21, 24)),
        ((2, 2), last(22, 25, 28, 31)),
    )

    def turn(n, carry):
        for i, (where, *moves) in enumerate(turns):

            @pl.when(n == i)
            def _():
                for move in moves:
                    move()
                stage(*where)

        attend()
        return carry

    lax.fori_loop(0, ROWS, turn, 0)

    def finish(p, carry):
        r = lax.div(order_ref[me * ROWS + p], ROWS)
        both = acc_ref[r]
        valid = t_ref[r] < total
        mixed = jnp.where(valid, both[:, :HD] / jnp.where(valid, both[:, HD:], 1.0), 0.0).astype(BF16)
        rows = pl.ds(pl.multiple_of(p * BLK, BLK), BLK)
        for g in range(4):
            att_ref[rows, g * HD : (g + 1) * HD] = mixed[g * BLK : (g + 1) * BLK, :]
        xperm_ref[rows, :] = xall[my_col, r]
        return carry

    half = FEAT // 2
    low, high = pl.ds(0, half), pl.ds(half, half)
    cols = (pl.ds(0, RUN // 2), pl.ds(RUN // 2, RUN // 2))

    def product(dx, core, h):
        rows = pl.ds(pl.multiple_of((wrap(x + dx) * 2 + core) * FEAT, FEAT), FEAT)
        return lax.dot_general(
            wo_all[rows, :], att_ref[cols[h], :], (((1,), (1,)), ((), ())), preferred_element_type=F32
        )

    lanes = ((0, low, xp), (0, high, xm), (1, high, xp), (2, low, xm), (1, low, xp), (2, high, xm))
    rings = [
        [
            pltpu.make_async_remote_copy(
                src_ref=ring_out.at[i, part, cols[h]], dst_ref=ring_in.at[i, part, cols[h]],
                send_sem=r_s.at[h, k], recv_sem=r_r.at[h, k], device_id=to, device_id_type=MESH,
            )
            for k, (i, part, to) in enumerate(lanes)
        ]
        for h in range(2)
    ]
    pairs = [
        [
            pltpu.make_async_remote_copy(
                src_ref=pair_out.at[i, :, cols[h]], dst_ref=pair_in.at[i, :, cols[h]],
                send_sem=p_s.at[h, i], recv_sem=p_r.at[h, i], device_id=sibling, device_id_type=MESH,
            )
            for i in range(4)
        ]
        for h in range(2)
    ]
    hops = (2, 1, 3, 0)

    def both(i, h):
        pairs[h][i].wait_recv()
        mine[i, :, cols[h]] = mine[i, :, cols[h]] + pair_in[i, :, cols[h]].astype(F32)

    def compute(i, h):
        pair_out[i, :, cols[h]] = product(hops[i], 1 - c, h).astype(BF16)
        pairs[h][i].start()
        mine[i, :, cols[h]] = product(hops[i], c, h)

    def emit(i, part, h, *ks):
        ring_out[i, part, cols[h]] = mine[i, part, cols[h]].astype(BF16)
        for k in ks:
            rings[h][k].start()

    def pass_on(h):
        for k, (i, part) in enumerate(((1, low), (2, high))):
            rings[h][k].wait_recv()
            mine[i, part, cols[h]] = mine[i, part, cols[h]] + ring_in[0, part, cols[h]].astype(F32)
            emit(i, part, h, 4 + k)

    wos.s5()
    for h in range(2):
        lax.fori_loop(8 * h, 8 * h + 8, finish, 0)
        compute(0, h)
        compute(1, h)
        both(0, h)
        ring_out[0, :, cols[h]] = mine[0, :, cols[h]].astype(BF16)
        rings[h][0].start()
        rings[h][1].start()
        compute(2, h)
        both(1, h)
        emit(1, high, h, 2)
        both(2, h)
        emit(2, low, h, 3)
    pass_on(0)
    compute(3, 0)
    compute(3, 1)
    pass_on(1)
    both(3, 0)
    both(3, 1)
    for i in range(4):
        columns = pl.ds(i * HD, HD)
        own[:, columns] = mine[3, :, columns] + xperm_ref[columns, :].T.astype(F32)

    orders = orderv_ref[...]
    holder = lax.broadcasted_iota(jnp.int32, (2, HD), 0) * 8 + lax.div(lax.broadcasted_iota(jnp.int32, (2, HD), 1), ROWS)
    for k in range(4):
        page = lax.fori_loop(
            0, 4 * ROWS, lambda p, found: found + jnp.where(page_ref[p] == me * 4 + k, p, 0), jnp.int32(0)
        )
        for i in range(4):
            block = page * 4 + i
            device = jnp.minimum(jnp.sum(jnp.where(orders == block, holder, 0)), ROWS - 1)
            run = jnp.minimum(lax.div(block, ROWS), ROWS - 1)
            cache_ref[k, 0, i * BLK : (i + 1) * BLK, :] = kv_ref[run, device]
    for h in range(2):
        for k in (2, 3, 4, 5):
            rings[h][k].wait_recv()
        arrived = ring_in[1, :, cols[h]].astype(F32) + ring_in[2, :, cols[h]].astype(F32)
        out_ref[:, cols[h]] = own[:, cols[h]] + arrived
    for copy in a2a + xout[0] + xout[1] + sout[0] + sout[1] + pairs[0] + pairs[1] + rings[0] + rings[1]:
        copy.wait_send()
    for spread in (wkv, wqs, wos, *kvs):
        spread.finish()


def layer(order, lengths, pages, packed, gain, query_gain, key_gain, w_query, w_key, w_value, w_out):
    vmem = pl.BlockSpec(memory_space=pltpu.VMEM)
    hbm = pl.BlockSpec(memory_space=pltpu.HBM)
    half = np.exp(np.arange(HD // 2, dtype=np.float64) * (-2.0 * THETA_LOG / HD)).astype(np.float32)
    freq = jnp.asarray(np.concatenate([half, half])[None, :])
    dma = pltpu.SemaphoreType.DMA
    return pl.pallas_call(
        layer_kernel,
        name="layer",
        out_shape=(
            jax.ShapeDtypeStruct((FEAT, RUN), F32),
            jax.ShapeDtypeStruct((4, 1, 4 * BLK, 2 * HD), BF16),
        ),
        in_specs=[hbm] * 13,
        out_specs=(vmem, vmem),
        scratch_shapes=[
            pltpu.SMEM((ROWS * ROWS,), jnp.int32), pltpu.SMEM((4,), jnp.int32), pltpu.SMEM((4 * ROWS,), jnp.int32),
            pltpu.VMEM((2, HD), jnp.int32),
            pltpu.VMEM((FEAT, RUN), BF16), pltpu.VMEM((ROWS, BLK, FEAT), BF16),
            pltpu.VMEM((COLS * FEAT // HD, HD), F32), pltpu.VMEM((COLS, FEAT), F32),
            pltpu.VMEM((1, HD), F32), pltpu.VMEM((1, HD), F32), pltpu.VMEM((1, HD), F32),
            pltpu.VMEM((ROWS, BLK, FEAT), BF16),
            pltpu.VMEM((COLS, ROWS, BLK, FEAT), BF16),
            pltpu.VMEM((COLS, RUN, FEAT), BF16),
            pltpu.VMEM((ROWS * WROW, 4 * HD), BF16),
            pltpu.VMEM((ROWS * WROW, 2 * HD), BF16),
            pltpu.VMEM((ROWS * WROW, 4 * HD), BF16),
            pltpu.VMEM((ROWS, ROWS, BLK, 2 * HD), BF16),
            pltpu.VMEM((ROWS, BLK, HD), F32),
            pltpu.VMEM((ROWS, BLK, HD), F32),
            pltpu.VMEM((ROWS, HD, HD), jnp.int32),
            pltpu.VMEM((ROWS, HD, HD), jnp.int32),
            pltpu.VMEM((8, RUN), jnp.int32),
            pltpu.VMEM((ROWS, HD, HD), BF16),
            pltpu.VMEM((RUN, HD), BF16),
            pltpu.VMEM((RUN, 2 * HD), BF16),
            pltpu.VMEM((ROWS, HD, 2 * HD), F32),
            pltpu.VMEM((RUN, 4 * HD), BF16),
            pltpu.VMEM((RUN, FEAT), BF16),
            pltpu.VMEM((4, FEAT, RUN), F32),
            pltpu.VMEM((FEAT, RUN), F32),
            pltpu.VMEM((4, FEAT, RUN), BF16),
            pltpu.VMEM((4, FEAT, RUN), BF16),
            pltpu.VMEM((3, FEAT, RUN), BF16),
            pltpu.VMEM((3, FEAT, RUN), BF16),
            dma((ROWS,)), dma((ROWS,)),
            dma((2, 8)), dma((2, 8)),
            dma((NCOPY,)), dma((NCOPY,)),
            dma((NCOPY,)), dma((NCOPY,)),
            dma((NCOPY,)), dma((NCOPY,)),
            dma((2, NCOPY)), dma((2, NCOPY)),
            dma((2, 4)), dma((2, 4)), dma((2, 6)), dma((2, 6)),
            dma((13,)),
        ],
        compiler_params=pltpu.CompilerParams(collective_id=0, has_side_effects=True, vmem_limit_bytes=44 << 20),
    )(*(pltpu.with_memory_space_constraint(a, pltpu.HBM) for a in (
        order, lengths, pages, order.reshape(2, HD), packed, gain, query_gain, key_gain, freq, w_query, w_key, w_value,
        w_out,
    )))


def per_device(
    packed, deal_order, lengths, segment_ids, page_table, attn_gain, query_gain, key_gain, w_query, w_key, w_value,
    w_out,
):
    hidden, cache = layer(
        deal_order, lengths, page_table, packed.T, attn_gain.reshape(COLS * FEAT // HD, HD),
        query_gain.reshape(1, HD), key_gain.reshape(1, HD), w_query, w_key, w_value, w_out.T,
    )
    return hidden.T, cache


def solution(mesh):
    in_specs = (
        P("row", "col"), P(), P(), P(), P(), P(), P(), P(),
        P("row", "col"), P("row", "col"), P("row", "col"), P("col", "row"),
    )
    out_specs = (P("row", "col"), P("row", "col", None, None))
    return jax.shard_map(per_device, mesh=mesh, in_specs=in_specs, out_specs=out_specs, check_vma=False)
```
